32 devices in a mesh: section: 4 (over y, x), seq: 8 (over z, core).
Axes of the slice: x: 2, y: 2, z: 4, core: 2. Of those that a mesh axis runs over, the one named last changes fastest.
Arguments:
- inflow: bfloat16 [4, 512, 4096], P('section', 'seq'), may hold values from -6 to 6
- fresh: bfloat16 [1, 512, 4096], P(None, 'seq'), may hold values from -6 to 6
- proj_weight: bfloat16 [4, 4096, 640], P('section'), may hold values from -0.09375 to 0.09375
- xz_weight: bfloat16 [4, 4096, 2, 4096], P('section', None, None, 'seq'), may hold values from -0.09375 to 0.09375
- conv_weight: float32 [4, 4, 4608], P('section'), may hold values from -3 to 3
- conv_bias: float32 [4, 4608], P('section'), may hold values from -3 to 3
- step_bias: float32 [4, 128], P('section'), may hold values from -3 to 0
- decay_log: float32 [4, 128], P('section'), may hold values from -7 to -1
- skip_weight: float32 [4, 128], P('section'), may hold values from 0.5 to 1.5
- norm_gain: float32 [4, 4096], P('section'), may hold values from 0.5 to 1.5
- out_weight: bfloat16 [4, 4096, 4096], P('section', 'seq'), may hold values from -0.09375 to 0.09375
Outputs:
- section_outputs: float32 [4, 2, 512, 4096], P('section', None, 'seq')
The draws below stay inside these ranges and needn't reach their ends.
All inputs are finite; a program needn't handle non-finite values.
Results may differ from the reference program's by a relative error of at most 0.014.
Values may be sent and summed in bfloat16 or wider, within the bound.
No kernel may reach another device: no remote copies, remote signals or barrier semaphores. Data moves between devices by JAX's collectives and lax.ppermute only.
A program may use at most 128 MiB of HBM per device.

```python
import jax
import jax.numpy as jnp
from jax import lax

D = 4096
HEADS = 128
HEAD_DIM = 32
STATE = 64
GROUPS = 4
CONV = 4
BLOCK = 128
WINDOW = 2
INNER = 4096
PROJ = 640
CONVCH = 4608
LENGTH = 512
SECTIONS = 4


def steps_of(stream_key, extent, split, least, high):
    def one(axis_at, parts):
        steps = jax.random.uniform(jax.random.fold_in(jax.random.fold_in(stream_key, 6), axis_at), (parts,), jnp.float32, least / len(split), high / len(split))
        return jnp.repeat(jnp.exp(steps), extent[axis_at] // parts).reshape((-1,) + (1,) * (len(extent) - axis_at - 1))

    factor_of = one(*split[0])
    for cut in split[1:]:
        factor_of = factor_of * one(*cut)
    return factor_of


def scatter_about(stream_key, extent, spread, bound, split=(), dtype=jnp.bfloat16):
    loudness = steps_of(stream_key, extent, split, -0.22, 0.18) if split else 1.0
    entries = jax.random.normal(stream_key, extent, jnp.float32) * spread * loudness
    return jnp.minimum(jnp.maximum(entries, -bound), bound).astype(dtype)


def setup_inputs(seed: int = 0) -> dict:
    arg_keys = jax.random.split(jax.random.key(seed), 12)
    return {
        "inflow": scatter_about(arg_keys[0], (SECTIONS, LENGTH, D), 1.0, 6.0, ((0, 4), (1, 8))),
        "fresh": scatter_about(arg_keys[1], (WINDOW - 1, LENGTH, D), 1.0, 6.0, ((1, 8),)),
        "proj_weight": scatter_about(arg_keys[2], (SECTIONS, D, PROJ), D ** -0.5, 0.09375, ((0, 4),)),
        "xz_weight": scatter_about(arg_keys[3], (SECTIONS, D, 2, INNER), D ** -0.5, 0.09375, ((0, 4), (3, 8))),
        "conv_weight": scatter_about(arg_keys[4], (SECTIONS, CONV, CONVCH), CONV ** -0.5, 3.0, ((0, 4),), jnp.float32),
        "conv_bias": scatter_about(arg_keys[5], (SECTIONS, CONVCH), 0.5, 3.0, ((0, 4),), jnp.float32),
        "step_bias": jnp.clip(-3.0 + 3.0 * jax.random.uniform(arg_keys[6], (SECTIONS, HEADS), jnp.float32) ** steps_of(arg_keys[6], (SECTIONS, HEADS), ((0, 4),), -0.2, 0.2), -3.0, 0.0),
        "decay_log": jnp.clip(-7.0 + 6.0 * jax.random.uniform(arg_keys[7], (SECTIONS, HEADS), jnp.float32) ** steps_of(arg_keys[7], (SECTIONS, HEADS), ((0, 4),), -0.2, 0.2), -7.0, -1.0),
        "skip_weight": jnp.clip(0.5 + 1.0 * jax.random.uniform(arg_keys[8], (SECTIONS, HEADS), jnp.float32) ** steps_of(arg_keys[8], (SECTIONS, HEADS), ((0, 4),), -0.2, 0.2), 0.5, 1.5),
        "norm_gain": jnp.clip(1.0 + 0.1 * jax.random.normal(arg_keys[9], (SECTIONS, INNER), jnp.float32), 0.5, 1.5),
        "out_weight": scatter_about(arg_keys[10], (SECTIONS, INNER, D), INNER ** -0.5, 0.09375, ((0, 4), (1, 8))),
    }


def block_terms(x_block, b_block, c_block, step_block, decay_block):
    cumulus = jnp.cumsum(decay_block, axis=0)
    scores = jnp.einsum('qgn,kgn->gqk', c_block.astype(jnp.float32), b_block.astype(jnp.float32))
    along = jnp.moveaxis(cumulus, 0, 2)
    row_count = cumulus.shape[0]
    row_index = lax.broadcasted_iota(jnp.int32, (row_count, row_count), 0)
    col_index = lax.broadcasted_iota(jnp.int32, (row_count, row_count), 1)
    log_gap = jnp.where(row_index >= col_index, along[..., :, None] - along[..., None, :], -1e+30)
    step_along = jnp.moveaxis(step_block, 0, 2)
    mixing = (scores[:, None] * jnp.exp(log_gap) * step_along[..., None, :]).astype(jnp.bfloat16)
    mixing = lax.optimization_barrier(mixing).astype(jnp.float32)
    diagonal_out = jnp.einsum('gjqk,kgjp->qgjp', mixing, x_block.astype(jnp.float32))
    block_total = cumulus[-1]
    weighted = (x_block.astype(jnp.float32) * (jnp.exp(block_total[None] - cumulus) * step_block)[..., None]).astype(jnp.bfloat16)
    weighted = lax.optimization_barrier(weighted).astype(jnp.float32)
    block_state = jnp.einsum('kgjp,kgn->gjpn', weighted, b_block.astype(jnp.float32))
    return (diagonal_out, cumulus, block_total, block_state)

def run_block(state, pieces):
    x_block, b_block, c_block, step_block, decay_block = pieces
    diagonal_out, cumulus, block_total, block_state = block_terms(x_block, b_block, c_block, step_block, decay_block)
    entering = lax.optimization_barrier(state.astype(jnp.bfloat16)).astype(jnp.float32)
    off_out = jnp.einsum('qgn,gjpn->qgjp', c_block.astype(jnp.float32), entering) * jnp.exp(cumulus)[..., None]
    new_state = jnp.exp(block_total)[..., None, None] * state + block_state
    return (new_state, diagonal_out + off_out)

def mamba_layer(layer_input, proj_w, xz_w, conv_taps, conv_offset, bias_steps, rate_log, skip_gain, out_gain, out_w):
    tokens = layer_input.shape[0]
    inner = HEADS * HEAD_DIM
    bc_width = GROUPS * STATE
    per_group = HEADS // GROUPS
    xz_both = jnp.dot(layer_input, xz_w.reshape(D, 2 * inner), preferred_element_type=jnp.float32).astype(jnp.bfloat16)
    projected = jnp.dot(layer_input, proj_w, preferred_element_type=jnp.float32).astype(jnp.bfloat16)
    joined = jnp.concatenate([xz_both[:, inner:], projected[:, :2 * bc_width]], axis=1)
    padded = jnp.concatenate([jnp.zeros((CONV - 1, joined.shape[1]), jnp.bfloat16), joined], axis=0)
    conv_sum = conv_offset + conv_taps[0] * padded[0:tokens].astype(jnp.float32)
    for offset in range(1, CONV):
        conv_sum = conv_sum + conv_taps[offset] * padded[offset:offset + tokens].astype(jnp.float32)
    convolved = jax.nn.silu(conv_sum).astype(jnp.bfloat16)
    block_count = tokens // BLOCK
    x_blocks = convolved[:, :inner].reshape(block_count, BLOCK, GROUPS, per_group, HEAD_DIM)
    b_blocks = convolved[:, inner:inner + bc_width].reshape(block_count, BLOCK, GROUPS, STATE)
    c_blocks = convolved[:, inner + bc_width:].reshape(block_count, BLOCK, GROUPS, STATE)
    step_size = jax.nn.softplus(projected[:, 2 * bc_width:].astype(jnp.float32) + bias_steps)
    log_decay = -jnp.exp(rate_log) * step_size
    step_blocks = step_size.reshape(block_count, BLOCK, GROUPS, per_group)
    decay_blocks = log_decay.reshape(block_count, BLOCK, GROUPS, per_group)
    start_state = jnp.zeros((GROUPS, per_group, HEAD_DIM, STATE), jnp.float32)
    _, scanned = lax.scan(run_block, start_state, (x_blocks, b_blocks, c_blocks, step_blocks, decay_blocks))
    x_heads = convolved[:, :inner].reshape(tokens, HEADS, HEAD_DIM).astype(jnp.float32)
    mixed = scanned.reshape(tokens, HEADS, HEAD_DIM) + skip_gain[:, None] * x_heads
    gated = mixed.reshape(tokens, inner) * jax.nn.silu(xz_both[:, :inner].astype(jnp.float32))
    grouped = gated.reshape(tokens, GROUPS, inner // GROUPS)
    mean_square = lax.optimization_barrier(jnp.mean(grouped * grouped, axis=2, keepdims=True))
    normed = ((grouped * lax.rsqrt(mean_square + 1e-05)).reshape(tokens, inner) * out_gain).astype(jnp.bfloat16)
    return jnp.dot(normed, out_w, preferred_element_type=jnp.float32)

def run_section(pieces):
    return mamba_layer(*pieces)

def reference(inflow, fresh, proj_weight, xz_weight, conv_weight, conv_bias, step_bias, decay_log, skip_weight, norm_gain, out_weight):
    params = (proj_weight, xz_weight, conv_weight, conv_bias, step_bias, decay_log, skip_weight, norm_gain, out_weight)
    current = inflow
    results = []
    for window_step in range(WINDOW):
        stacked = lax.map(run_section, (current,) + params)
        results.append(stacked)
        if window_step + 1 < WINDOW:
            current = jnp.concatenate([fresh[window_step][None], stacked[:-1].astype(jnp.bfloat16)], axis=0)
    return jnp.stack(results, axis=1)
```

```python
import functools

import jax
import jax.numpy as jnp
from jax import lax
from jax.experimental import pallas as pl
from jax.experimental.pallas import tpu as pltpu
from jax.sharding import PartitionSpec as P

HEADS = 128
HEAD_DIM = 32
STATE = 64
GROUPS = 4
CONV = 4
BLOCK = 128
LANES = 128
PIECES = 2
QUAD = LANES // HEAD_DIM


bf16 = jnp.bfloat16
f32 = jnp.float32


def swapped(value, bit):
    count = lax.axis_size("seq")
    return lax.ppermute(value, "seq", [(i, i ^ bit) for i in range(count)])


def chip_ring(value):
    count = lax.axis_size("seq")
    return lax.ppermute(value, "seq", [(i, (i + 2) % count) for i in range(count)])


def next_section(value, chips_on):
    sections, count = lax.axis_size("section"), lax.axis_size("seq")
    pairs = [
        (s * count + i, (s + 1) % sections * count + (i + 2 * chips_on) % count)
        for s in range(sections)
        for i in range(count)
    ]
    return lax.ppermute(value, ("section", "seq"), pairs)


def project_kernel(where_ref, *refs):
    del where_ref
    xs, refs = refs[: 2 * PIECES], refs[2 * PIECES :]
    w_mine, w_other, p_mine, p_other = refs[:4]
    out_xz, out_p = refs[-2:]
    mine = [x[...] for x in xs[:PIECES]]
    other = [x[...] for x in xs[PIECES:]]

    def product(first, second):
        total = None
        for pieces, weight in ((mine, first), (other, second)):
            depth = pieces[0].shape[1]
            for i, piece in enumerate(pieces):
                part = jnp.dot(
                    piece, weight[i * depth : (i + 1) * depth, :], preferred_element_type=f32
                )
                total = part if total is None else total + part
        return total.astype(bf16)

    out_xz[...] = product(w_mine, w_other)

    @pl.when(pl.program_id(0) == 0)
    def _():
        out_p[...] = product(p_mine, p_other)


def project(where, mine, other, xz_weight, p_weight, length, buffers):
    rows, depth = mine[0].shape
    width, n_xz = xz_weight.shape
    n_p = p_weight.shape[1]
    tile = 256
    half = width // 2
    xs = list(mine) + list(other)
    in_specs = [pl.BlockSpec((rows, depth), lambda j, w: (0, 0)) for _ in xs] + [
        pl.BlockSpec((half, tile), lambda j, w: (w[1], j)),
        pl.BlockSpec((half, tile), lambda j, w: (1 - w[1], j)),
        pl.BlockSpec((half, n_p), lambda j, w: (w[1], 0)),
        pl.BlockSpec((half, n_p), lambda j, w: (1 - w[1], 0)),
    ]
    args = xs + [xz_weight, xz_weight, p_weight, p_weight]
    aliases = {}
    if buffers is not None:
        aliases = {1 + len(args): 0, 2 + len(args): 1}
        in_specs += [pl.BlockSpec(memory_space=pl.ANY)] * 2
        args += list(buffers)
    return pl.pallas_call(
        project_kernel,
        grid_spec=pltpu.PrefetchScalarGridSpec(
            num_scalar_prefetch=1,
            grid=(n_xz // tile,),
            in_specs=in_specs,
            out_specs=[
                pl.BlockSpec((rows, tile), lambda j, w: (w[0], j)),
                pl.BlockSpec((rows, n_p), lambda j, w: (w[0], 0)),
            ],
        ),
        out_shape=[
            jax.ShapeDtypeStruct((length, n_xz), bf16),
            jax.ShapeDtypeStruct((length, n_p), bf16),
        ],
        input_output_aliases=aliases,
        cost_estimate=pl.CostEstimate(
            flops=2 * rows * width * (n_xz + n_p),
            bytes_accessed=2 * width * (n_xz + n_p),
            transcendentals=0,
        ),
        name="project",
    )(where, *args)


def silu(value):
    return value / (1.0 + jnp.exp(-value))


def mix_kernel(
    xz_ref, p_ref, taps_ref, offset_ref, bias_ref, rate_ref, skip_ref, gain_ref,
    out_ref, squares_ref, padded_ref, state_ref,
):
    chans = out_ref.shape[1]
    heads = chans // HEAD_DIM
    lead = 8

    @pl.when(pl.program_id(0) == 0)
    def _():
        padded_ref[0:lead, :] = jnp.zeros((lead, padded_ref.shape[1]), f32)
        state_ref[...] = jnp.zeros_like(state_ref)

    padded_ref[lead : lead + BLOCK, 0:chans] = xz_ref[:, chans:].astype(f32)
    padded_ref[lead : lead + BLOCK, chans:] = p_ref[:, 0 : 2 * STATE].astype(f32)
    total = offset_ref[0:1, :]
    for k in range(CONV):
        start = lead - (CONV - 1) + k
        total = total + taps_ref[k : k + 1, :] * padded_ref[start : start + BLOCK, :]
    padded_ref[0:lead, :] = padded_ref[BLOCK : BLOCK + lead, :]
    convolved = silu(total).astype(bf16)
    x = convolved[:, :chans]
    bc = convolved[:, chans:]
    b = bc[:, :STATE]
    c = bc[:, STATE:]

    step = jax.nn.softplus(p_ref[:, 2 * STATE :].astype(f32) + bias_ref[0:1, :])
    decay = rate_ref[0:1, :] * step
    row = lax.broadcasted_iota(jnp.int32, (BLOCK, BLOCK), 0)
    col = lax.broadcasted_iota(jnp.int32, (BLOCK, BLOCK), 1)
    lower = row >= col
    cumulus = jnp.dot(
        lower.astype(f32), decay, precision=lax.Precision.HIGHEST, preferred_element_type=f32
    )
    block_total = cumulus[BLOCK - 1 : BLOCK, :]
    cumulus_t = cumulus.T
    step_t = step.T
    scores = lax.dot_general(c, b, (((1,), (1,)), ((), ())), preferred_element_type=f32)
    spread = (
        lax.broadcasted_iota(jnp.int32, (LANES, chans), 0)
        == lax.broadcasted_iota(jnp.int32, (LANES, chans), 1) // HEAD_DIM
    ).astype(f32)

    def per_channel(table):
        return jnp.dot(
            table, spread, precision=lax.Precision.HIGHEST, preferred_element_type=f32
        )

    grown = per_channel(jnp.exp(cumulus))
    kept = per_channel(jnp.exp(block_total - cumulus) * step)
    x_wide = x.astype(f32)
    weighted = (x_wide * kept).astype(bf16)
    entering = state_ref[...].astype(bf16)
    carried = jnp.dot(c, entering, preferred_element_type=f32) * grown
    block_state = lax.dot_general(
        b, weighted, (((0,), (0,)), ((), ())), preferred_element_type=f32
    )
    state_ref[...] = grown[BLOCK - 1 : BLOCK, :] * state_ref[...] + block_state

    lane_head = lax.broadcasted_iota(jnp.int32, (BLOCK, LANES), 1) // HEAD_DIM
    squares = jnp.zeros((BLOCK, 1), f32)
    for quad in range(heads // QUAD):
        lanes = slice(quad * LANES, (quad + 1) * LANES)
        x_quad = x[:, lanes]
        left, right = [], []
        for j in range(QUAD):
            h = quad * QUAD + j
            gap = jnp.where(lower, cumulus[:, h : h + 1] - cumulus_t[h : h + 1, :], -1e30)
            left.append((scores * jnp.exp(gap) * step_t[h : h + 1, :]).astype(bf16))
            right.append(jnp.where(lane_head == j, x_quad, jnp.zeros_like(x_quad)))
        diagonal = jnp.dot(
            jnp.concatenate(left, axis=1),
            jnp.concatenate(right, axis=0),
            preferred_element_type=f32,
        )
        mixed = diagonal + carried[:, lanes] + skip_ref[0:1, lanes] * x_wide[:, lanes]
        gated = mixed * silu(xz_ref[:, lanes].astype(f32))
        squares = squares + jnp.sum(gated * gated, axis=1, keepdims=True)
        out_ref[:, lanes] = (gated * gain_ref[0:1, lanes]).astype(bf16)
    squares_ref[...] = jnp.broadcast_to(squares, squares_ref.shape)


def mix(xz, p, tables):
    length, both = xz.shape
    chans = both // 2
    n_p = p.shape[1]
    whole = lambda table: pl.BlockSpec(table.shape, lambda i: (0, 0))
    return pl.pallas_call(
        mix_kernel,
        grid=(length // BLOCK,),
        in_specs=[
            pl.BlockSpec((BLOCK, both), lambda i: (i, 0)),
            pl.BlockSpec((BLOCK, n_p), lambda i: (i, 0)),
        ]
        + [whole(table) for table in tables],
        out_specs=[
            pl.BlockSpec((BLOCK, chans), lambda i: (i, 0)),
            pl.BlockSpec((BLOCK, LANES), lambda i: (i, 0)),
        ],
        out_shape=[
            jax.ShapeDtypeStruct((length, chans), bf16),
            jax.ShapeDtypeStruct((length, LANES), f32),
        ],
        scratch_shapes=[
            pltpu.VMEM((BLOCK + 8, chans + 2 * STATE), f32),
            pltpu.VMEM((STATE, chans), f32),
        ],
        cost_estimate=pl.CostEstimate(
            flops=2 * length * chans * BLOCK * 8,
            bytes_accessed=2 * length * (both + chans + n_p),
            transcendentals=length * chans * 4,
        ),
        name="mix",
    )(xz, p, *tables)


def out_kernel(where_ref, g_mine, g_other, squares, w_mine, w_other, *outs, scale):
    del where_ref
    rate = lax.rsqrt(squares[:, 0:1] * scale + 1e-05)
    tile = outs[0].shape[1]
    for i, out in enumerate(outs):
        cols = slice(i * tile, (i + 1) * tile)
        part = jnp.dot(g_mine[...], w_mine[:, cols], preferred_element_type=f32)
        part = part + jnp.dot(g_other[...], w_other[:, cols], preferred_element_type=f32)
        out[...] = (part * rate).astype(out.dtype)


def out_project(where, g_mine, g_other, squares, w_mine, w_other, rows, dtype):
    chans, cols = w_mine.shape
    tile = cols // PIECES
    at = lambda width: pl.BlockSpec((rows, width), lambda i, w: (w[0], 0))
    weight = pl.BlockSpec((chans, cols), lambda i, w: (0, 0))
    return pl.pallas_call(
        functools.partial(out_kernel, scale=GROUPS / (HEADS * HEAD_DIM)),
        grid_spec=pltpu.PrefetchScalarGridSpec(
            num_scalar_prefetch=1,
            grid=(1,),
            in_specs=[at(chans), at(chans), at(LANES), weight, weight],
            out_specs=[pl.BlockSpec((rows, tile), lambda i, w: (0, 0))] * PIECES,
        ),
        out_shape=[jax.ShapeDtypeStruct((rows, tile), dtype)] * PIECES,
        cost_estimate=pl.CostEstimate(
            flops=4 * rows * chans * cols, bytes_accessed=4 * chans * cols, transcendentals=0
        ),
        name="out_project",
    )(where, g_mine, g_other, squares, w_mine, w_other)


def on_device(
    inflow,
    fresh,
    proj_weight,
    xz_weight,
    conv_weight,
    conv_bias,
    step_bias,
    decay_log,
    skip_weight,
    norm_gain,
    out_weight,
):
    members = lax.axis_size("seq")
    sections = lax.axis_size("section")
    position = lax.axis_index("section")
    member = lax.axis_index("seq")
    core = member % 2
    chip = member // 2
    chips = members // 2
    tokens, width = inflow.shape[1], inflow.shape[2]
    length = tokens * members
    rows = 2 * tokens
    half = width // 2
    piece = half // PIECES
    inner = HEADS * HEAD_DIM
    heads_dev = HEADS // members
    chan_dev = heads_dev * HEAD_DIM
    bc_width = GROUPS * STATE
    per_group = HEADS // GROUPS
    group_members = members // GROUPS
    head_start = member * heads_dev
    group_index = head_start // per_group
    b_start = group_index * STATE
    c_start = bc_width + group_index * STATE
    dt_start = 2 * bc_width + head_start

    def half_columns(shard):
        mine = lax.dynamic_slice_in_dim(shard, core * half, half, 1)
        theirs = lax.dynamic_slice_in_dim(shard, (1 - core) * half, half, 1)
        got = swapped(theirs, 1)
        first = jnp.where(core == 0, mine, got)
        second = jnp.where(core == 0, got, mine)
        both = jnp.concatenate([first, second], axis=0)
        return [both[:, i * piece : (i + 1) * piece] for i in range(PIECES)]

    entering = half_columns(inflow[0])

    xz_local = xz_weight[0].reshape(width, 2 * chan_dev)
    full_proj = proj_weight[0]
    p_local = jnp.concatenate(
        [
            lax.dynamic_slice_in_dim(full_proj, b_start, STATE, 1),
            lax.dynamic_slice_in_dim(full_proj, c_start, STATE, 1),
            lax.dynamic_slice_in_dim(full_proj, dt_start, heads_dev, 1),
            jnp.zeros((width, LANES - heads_dev), bf16),
        ],
        axis=1,
    )

    def own_channels(table):
        return jnp.concatenate(
            [
                lax.dynamic_slice_in_dim(table, head_start * HEAD_DIM, chan_dev, 1),
                lax.dynamic_slice_in_dim(table, inner + b_start, STATE, 1),
                lax.dynamic_slice_in_dim(table, inner + c_start, STATE, 1),
            ],
            axis=1,
        )

    def own_heads(table):
        return lax.dynamic_slice_in_dim(table, head_start, heads_dev, 1)

    def to_lanes(table):
        return jnp.pad(table, ((0, 0), (0, LANES - table.shape[1])))

    tables = (
        own_channels(conv_weight[0]),
        own_channels(conv_bias),
        to_lanes(own_heads(step_bias)),
        to_lanes(-jnp.exp(own_heads(decay_log))),
        jnp.repeat(own_heads(skip_weight), HEAD_DIM, axis=1),
        lax.dynamic_slice_in_dim(norm_gain, head_start * HEAD_DIM, chan_dev, 1),
    )
    out_local = out_weight[0]
    w_mine = lax.dynamic_slice_in_dim(out_local, core * half, half, 1)
    w_other = swapped(lax.dynamic_slice_in_dim(out_local, (1 - core) * half, half, 1), 1)

    def at_chip(steps):
        return jnp.stack([(chip - steps) % chips, core]).astype(jnp.int32)

    def layer(held, arriving):
        buffers = None
        for step in range(chips):
            if step == 1:
                held = arriving
            elif step > 1:
                held = [chip_ring(part) for part in held]
            other = [swapped(part, 1) for part in held]
            buffers = project(
                at_chip(step), held, other, xz_local, p_local, length, buffers
            )
        gated, squares = mix(*buffers, tables)
        gated_other = swapped(gated, 1)
        bit = 1
        while bit < group_members:
            squares = squares + swapped(squares, bit)
            bit *= 2
        running = None
        for step in range(1, chips + 1):
            parts = out_project(
                at_chip(step),
                gated,
                gated_other,
                squares,
                w_mine,
                w_other,
                rows,
                bf16 if step == 1 else f32,
            )
            if running is not None:
                parts = [part + came.astype(f32) for part, came in zip(parts, running)]
            if step < chips:
                running = [chip_ring(part.astype(bf16)) for part in parts]
        return parts

    def own_tokens(parts):
        both = jnp.concatenate(parts, axis=1)
        mine = lax.dynamic_slice_in_dim(both, core * tokens, tokens, 0)
        theirs = lax.dynamic_slice_in_dim(both, (1 - core) * tokens, tokens, 0)
        got = swapped(theirs, 1)
        return jnp.where(
            core == 0,
            jnp.concatenate([mine, got], axis=1),
            jnp.concatenate([got, mine], axis=1),
        )

    first = layer(entering, [chip_ring(part) for part in entering])
    fresh_parts = half_columns(fresh[0])
    leaving = [
        jnp.where(position == sections - 1, new, part.astype(bf16))
        for new, part in zip(fresh_parts, first)
    ]
    second = layer(
        [next_section(part, 0) for part in leaving], [next_section(part, 1) for part in leaving]
    )
    return jnp.stack([own_tokens(first), own_tokens(second)])[None]


def solution(mesh):
    placed = (
        P("section", "seq", None),
        P(None, "seq", None),
        P("section", None, None),
        P("section", None, None, "seq"),
        P("section", None, None),
        P("section", None),
        P("section", None),
        P("section", None),
        P("section", None),
        P("section", None),
        P("section", "seq", None),
    )
    return jax.shard_map(
        on_device,
        mesh=mesh,
        in_specs=placed,
        out_specs=P("section", None, "seq", None),
        check_vma=False,
    )
```

```python
import functools

import jax
import jax.numpy as jnp
from jax import lax
from jax.experimental import pallas as pl
from jax.experimental.pallas import tpu as pltpu
from jax.sharding import PartitionSpec as P

HEADS = 128
HEAD_DIM = 32
STATE = 64
GROUPS = 4
CONV = 4
BLOCK = 128
LANES = 128
PIECES = 2
QUAD = LANES // HEAD_DIM


bf16 = jnp.bfloat16
f32 = jnp.float32


def swapped(value, bit):
    count = lax.axis_size("seq")
    return lax.ppermute(value, "seq", [(i, i ^ bit) for i in range(count)])


def chip_ring(value):
    count = lax.axis_size("seq")
    return lax.ppermute(value, "seq", [(i, (i + 2) % count) for i in range(count)])


def next_section(value, chips_on):
    sections, count = lax.axis_size("section"), lax.axis_size("seq")
    pairs = [
        (s * count + i, (s + 1) % sections * count + (i + 2 * chips_on) % count)
        for s in range(sections)
        for i in range(count)
    ]
    return lax.ppermute(value, ("section", "seq"), pairs)


IN_VMEM = pl.BlockSpec(memory_space=pltpu.VMEM)
IN_SMEM = pl.BlockSpec(memory_space=pltpu.SMEM)
PARAMS = pltpu.CompilerParams(vmem_limit_bytes=16 * 1024 * 1024)


def after(values, *others):
    return lax.optimization_barrier((values, others))[0]


def chip_at(where, steps, chips):
    return lax.rem(where[0] + (chips - steps), chips)


def project_kernel(where, *refs, steps, chips, by_rows):
    xs, refs = refs[: 2 * PIECES], refs[2 * PIECES :]
    weights, outs = refs[:2], refs[-2:]
    core = where[1]
    rows = outs[0].shape[0] // chips
    start = chip_at(where, steps, chips) * rows
    if by_rows:
        tokens = rows // 2
        tall = jnp.concatenate([x[...] for x in xs], axis=0)
        mine = pl.ds(pl.multiple_of(start + core * tokens, tokens), tokens)
        other = pl.ds(pl.multiple_of(start + (1 - core) * tokens, tokens), tokens)
        for weight, out in zip(weights, outs):
            total = jnp.dot(tall, weight[...], preferred_element_type=f32).astype(bf16)
            out[mine, :] = total[:tokens]
            out[other, :] = total[tokens:]
        return
    depth = xs[0].shape[1]
    for weight, out in zip(weights, outs):
        total = None
        for i, x in enumerate(xs):
            at_core = core if i < PIECES else 1 - core
            at = pl.multiple_of((at_core * PIECES + i % PIECES) * depth, depth)
            part = jnp.dot(x[...], weight[pl.ds(at, depth), :], preferred_element_type=f32)
            total = part if total is None else total + part
        out[pl.ds(pl.multiple_of(start, rows), rows), :] = total.astype(bf16)


def project(where, steps, chips, xs, weights, length, buffers, by_rows):
    args = [where, *xs, *weights]
    in_specs = [IN_SMEM] + [IN_VMEM] * (len(args) - 1)
    aliases = {}
    if buffers is not None:
        aliases = {len(args): 0, len(args) + 1: 1}
        args += list(buffers)
        in_specs += [IN_VMEM] * 2
    width = weights[0].shape[0]
    columns = sum(weight.shape[1] for weight in weights)
    return pl.pallas_call(
        functools.partial(project_kernel, steps=steps, chips=chips, by_rows=by_rows),
        in_specs=in_specs,
        out_specs=[IN_VMEM] * 2,
        out_shape=[jax.ShapeDtypeStruct((length, weight.shape[1]), bf16) for weight in weights],
        input_output_aliases=aliases,
        compiler_params=PARAMS,
        cost_estimate=pl.CostEstimate(
            flops=2 * (length // chips) * width * columns,
            bytes_accessed=2 * width * columns,
            transcendentals=0,
        ),
        name="project",
    )(*args)


def silu(value):
    return value / (1.0 + jnp.exp(-value))


def mix_kernel(
    xz_ref, p_ref, taps_ref, offset_ref, bias_ref, rate_ref, skip_ref, gain_ref,
    out_ref, squares_ref, padded_ref, state_ref,
):
    chans = out_ref.shape[1]
    heads = chans // HEAD_DIM
    lead = 8
    rows = pl.ds(pl.multiple_of(pl.program_id(0) * BLOCK, BLOCK), BLOCK)

    @pl.when(pl.program_id(0) == 0)
    def _():
        padded_ref[0:lead, :] = jnp.zeros((lead, padded_ref.shape[1]), f32)
        state_ref[...] = jnp.zeros_like(state_ref)

    padded_ref[lead : lead + BLOCK, 0:chans] = xz_ref[rows, chans:].astype(f32)
    padded_ref[lead : lead + BLOCK, chans:] = p_ref[rows, 0 : 2 * STATE].astype(f32)
    total = offset_ref[0:1, :]
    for k in range(CONV):
        start = lead - (CONV - 1) + k
        total = total + taps_ref[k : k + 1, :] * padded_ref[start : start + BLOCK, :]
    padded_ref[0:lead, :] = padded_ref[BLOCK : BLOCK + lead, :]
    convolved = silu(total).astype(bf16)
    x = convolved[:, :chans]
    bc = convolved[:, chans:]
    b = bc[:, :STATE]
    c = bc[:, STATE:]

    step = jax.nn.softplus(p_ref[rows, 2 * STATE :].astype(f32) + bias_ref[0:1, :])
    decay = rate_ref[0:1, :] * step
    row = lax.broadcasted_iota(jnp.int32, (BLOCK, BLOCK), 0)
    col = lax.broadcasted_iota(jnp.int32, (BLOCK, BLOCK), 1)
    lower = row >= col
    cumulus = jnp.dot(
        lower.astype(f32), decay, precision=lax.Precision.HIGHEST, preferred_element_type=f32
    )
    block_total = cumulus[BLOCK - 1 : BLOCK, :]
    cumulus_t = cumulus.T
    step_t = step.T
    scores = lax.dot_general(c, b, (((1,), (1,)), ((), ())), preferred_element_type=f32)
    spread = (
        lax.broadcasted_iota(jnp.int32, (LANES, chans), 0)
        == lax.broadcasted_iota(jnp.int32, (LANES, chans), 1) // HEAD_DIM
    ).astype(f32)

    def per_channel(table):
        return jnp.dot(
            table, spread, precision=lax.Precision.HIGHEST, preferred_element_type=f32
        )

    grown = per_channel(jnp.exp(cumulus))
    kept = per_channel(jnp.exp(block_total - cumulus) * step)
    x_wide = x.astype(f32)
    weighted = (x_wide * kept).astype(bf16)
    entering = state_ref[...].astype(bf16)
    carried = jnp.dot(c, entering, preferred_element_type=f32) * grown
    block_state = lax.dot_general(
        b, weighted, (((0,), (0,)), ((), ())), preferred_element_type=f32
    )
    state_ref[...] = grown[BLOCK - 1 : BLOCK, :] * state_ref[...] + block_state

    lane_head = lax.broadcasted_iota(jnp.int32, (BLOCK, LANES), 1) // HEAD_DIM
    squares = jnp.zeros((BLOCK, 1), f32)
    for quad in range(heads // QUAD):
        lanes = slice(quad * LANES, (quad + 1) * LANES)
        x_quad = x[:, lanes]
        left, right = [], []
        for j in range(QUAD):
            h = quad * QUAD + j
            gap = jnp.where(lower, cumulus[:, h : h + 1] - cumulus_t[h : h + 1, :], -1e30)
            left.append((scores * jnp.exp(gap) * step_t[h : h + 1, :]).astype(bf16))
            right.append(jnp.where(lane_head == j, x_quad, jnp.zeros_like(x_quad)))
        diagonal = jnp.dot(
            jnp.concatenate(left, axis=1),
            jnp.concatenate(right, axis=0),
            preferred_element_type=f32,
        )
        mixed = diagonal + carried[:, lanes] + skip_ref[0:1, lanes] * x_wide[:, lanes]
        gated = mixed * silu(xz_ref[rows, lanes].astype(f32))
        squares = squares + jnp.sum(gated * gated, axis=1, keepdims=True)
        out_ref[rows, lanes] = (gated * gain_ref[0:1, lanes]).astype(bf16)
    squares_ref[rows, :] = jnp.broadcast_to(squares, (BLOCK, LANES))


def mix(xz, p, tables):
    length, both = xz.shape
    chans = both // 2
    n_p = p.shape[1]
    return pl.pallas_call(
        mix_kernel,
        grid=(length // BLOCK,),
        in_specs=[IN_VMEM] * (2 + len(tables)),
        out_specs=[IN_VMEM] * 2,
        compiler_params=PARAMS,
        out_shape=[
            jax.ShapeDtypeStruct((length, chans), bf16),
            jax.ShapeDtypeStruct((length, LANES), f32),
        ],
        scratch_shapes=[
            pltpu.VMEM((BLOCK + 8, chans + 2 * STATE), f32),
            pltpu.VMEM((STATE, chans), f32),
        ],
        cost_estimate=pl.CostEstimate(
            flops=2 * length * chans * BLOCK * 8,
            bytes_accessed=2 * length * (both + chans + n_p),
            transcendentals=length * chans * 4,
        ),
        name="mix",
    )(xz, p, *tables)


def out_kernel(where, g_mine, g_other, w_mine, w_other, *refs, steps, chips, scale):
    squares, outs = refs[:-PIECES], refs[-PIECES:]
    rows, tile = outs[0].shape
    at = pl.ds(pl.multiple_of(chip_at(where, steps, chips) * rows, rows), rows)
    total = squares[0][at, 0:1]
    for more in squares[1:]:
        total = total + more[at, 0:1]
    rate = lax.rsqrt(total * scale + 1e-05)
    for i, out in enumerate(outs):
        cols = slice(i * tile, (i + 1) * tile)
        part = jnp.dot(g_mine[at, :], w_mine[:, cols], preferred_element_type=f32)
        part = part + jnp.dot(g_other[at, :], w_other[:, cols], preferred_element_type=f32)
        out[...] = (part * rate).astype(out.dtype)


def out_project(where, steps, chips, gated, weights, squares, rows, dtype):
    chans, cols = weights[0].shape
    args = [where, *gated, *weights, *squares]
    return pl.pallas_call(
        functools.partial(
            out_kernel, steps=steps, chips=chips, scale=GROUPS / (HEADS * HEAD_DIM)
        ),
        in_specs=[IN_SMEM] + [IN_VMEM] * (len(args) - 1),
        out_specs=[IN_VMEM] * PIECES,
        out_shape=[jax.ShapeDtypeStruct((rows, cols // PIECES), dtype)] * PIECES,
        compiler_params=PARAMS,
        cost_estimate=pl.CostEstimate(
            flops=4 * rows * chans * cols, bytes_accessed=4 * chans * cols, transcendentals=0
        ),
        name="out_project",
    )(*args)


def on_device(
    inflow,
    fresh,
    proj_weight,
    xz_weight,
    conv_weight,
    conv_bias,
    step_bias,
    decay_log,
    skip_weight,
    norm_gain,
    out_weight,
):
    members = lax.axis_size("seq")
    sections = lax.axis_size("section")
    position = lax.axis_index("section")
    member = lax.axis_index("seq")
    core = member % 2
    chip = member // 2
    chips = members // 2
    tokens, width = inflow.shape[1], inflow.shape[2]
    length = tokens * members
    rows = 2 * tokens
    half = width // 2
    piece = half // PIECES
    inner = HEADS * HEAD_DIM
    heads_dev = HEADS // members
    chan_dev = heads_dev * HEAD_DIM
    bc_width = GROUPS * STATE
    per_group = HEADS // GROUPS
    group_members = members // GROUPS
    head_start = member * heads_dev
    group_index = head_start // per_group
    b_start = group_index * STATE
    c_start = bc_width + group_index * STATE
    dt_start = 2 * bc_width + head_start

    def half_columns(shard):
        mine = lax.dynamic_slice_in_dim(shard, core * half, half, 1)
        theirs = lax.dynamic_slice_in_dim(shard, (1 - core) * half, half, 1)
        got = swapped(theirs, 1)
        first = jnp.where(core == 0, mine, got)
        second = jnp.where(core == 0, got, mine)
        both = jnp.concatenate([first, second], axis=0)
        return [both[:, i * piece : (i + 1) * piece] for i in range(PIECES)]

    shard = inflow[0]
    entering = [
        shard[i * tokens // PIECES : (i + 1) * tokens // PIECES] for i in range(PIECES)
    ]
    arriving = [chip_ring(part) for part in entering]

    xz_local = xz_weight[0].reshape(width, 2 * chan_dev)
    full_proj = proj_weight[0]
    p_local = jnp.concatenate(
        [
            lax.dynamic_slice_in_dim(full_proj, b_start, STATE, 1),
            lax.dynamic_slice_in_dim(full_proj, c_start, STATE, 1),
            lax.dynamic_slice_in_dim(full_proj, dt_start, heads_dev, 1),
            jnp.zeros((width, LANES - heads_dev), bf16),
        ],
        axis=1,
    )

    def own_channels(table):
        return jnp.concatenate(
            [
                lax.dynamic_slice_in_dim(table, head_start * HEAD_DIM, chan_dev, 1),
                lax.dynamic_slice_in_dim(table, inner + b_start, STATE, 1),
                lax.dynamic_slice_in_dim(table, inner + c_start, STATE, 1),
            ],
            axis=1,
        )

    def own_heads(table):
        return lax.dynamic_slice_in_dim(table, head_start, heads_dev, 1)

    def to_lanes(table):
        return jnp.pad(table, ((0, 0), (0, LANES - table.shape[1])))

    tables = (
        own_channels(conv_weight[0]),
        own_channels(conv_bias),
        to_lanes(own_heads(step_bias)),
        to_lanes(-jnp.exp(own_heads(decay_log))),
        jnp.repeat(own_heads(skip_weight), HEAD_DIM, axis=1),
        lax.dynamic_slice_in_dim(norm_gain, head_start * HEAD_DIM, chan_dev, 1),
    )
    where = jnp.stack([chip, core]).astype(jnp.int32)

    def layer(held, arriving, out_weights, by_rows):
        buffers = None
        before = None
        for step in range(chips):
            if step == 1:
                held = arriving
            elif step == 2 and by_rows:
                held = [chip_ring(part) for part in after(held, xz_local)]
            elif step > 1:
                held = [chip_ring(part) for part in (after(held, before) if step > 2 else held)]
            other = [swapped(part, 1) for part in held]
            before = buffers
            buffers = project(
                where, step, chips, held + other, (xz_local, p_local), length, buffers, by_rows
            )
        gated, squares = mix(*buffers, tables)
        gated_both = (gated, swapped(gated, 1))
        squares_all = [squares] + [swapped(squares, mask) for mask in range(1, group_members)]
        running = None
        for step in range(1, chips + 1):
            parts = out_project(
                where,
                step,
                chips,
                gated_both,
                out_weights,
                squares_all,
                rows,
                bf16 if step == 1 else f32,
            )
            if running is not None:
                parts = [part + came.astype(f32) for part, came in zip(parts, running)]
            if step < chips:
                running = [chip_ring(part.astype(bf16)) for part in parts]
        return parts

    def own_tokens(parts):
        both = jnp.concatenate(parts, axis=1)
        mine = lax.dynamic_slice_in_dim(both, core * tokens, tokens, 0)
        theirs = lax.dynamic_slice_in_dim(both, (1 - core) * tokens, tokens, 0)
        got = swapped(theirs, 1)
        return jnp.where(
            core == 0,
            jnp.concatenate([mine, got], axis=1),
            jnp.concatenate([got, mine], axis=1),
        )

    out_local = after(out_weight[0], arriving)
    w_mine = lax.dynamic_slice_in_dim(out_local, core * half, half, 1)
    w_other = swapped(lax.dynamic_slice_in_dim(out_local, (1 - core) * half, half, 1), 1)
    first = layer(entering, arriving, (w_mine, w_other), True)
    fresh_parts = half_columns(after(fresh[0], arriving))
    leaving = [
        jnp.where(position == sections - 1, new, part.astype(bf16))
        for new, part in zip(fresh_parts, first)
    ]
    second = layer(
        [next_section(part, 0) for part in leaving],
        [next_section(part, 1) for part in leaving],
        (w_mine, w_other),
        False,
    )
    return jnp.stack([own_tokens(first), own_tokens(second)])[None]


def solution(mesh):
    placed = (
        P("section", "seq", None),
        P(None, "seq", None),
        P("section", None, None),
        P("section", None, None, "seq"),
        P("section", None, None),
        P("section", None),
        P("section", None),
        P("section", None),
        P("section", None),
        P("section", None),
        P("section", "seq", None),
    )
    return jax.shard_map(
        on_device,
        mesh=mesh,
        in_specs=placed,
        out_specs=P("section", None, "seq", None),
        check_vma=False,
    )
```

```python
import functools

import jax
import jax.numpy as jnp
from jax import lax
from jax.experimental import pallas as pl
from jax.experimental.pallas import tpu as pltpu
from jax.sharding import PartitionSpec as P


HEADS = 128
HEAD_DIM = 32
STATE = 64
GROUPS = 4
CONV = 4
BLOCK = 128
LANES = 128
PIECES = 2
QUAD = LANES // HEAD_DIM


bf16 = jnp.bfloat16
f32 = jnp.float32


def swapped(value, bit):
    count = lax.axis_size("seq")
    return lax.ppermute(value, "seq", [(i, i ^ bit) for i in range(count)])


def chip_ring(value):
    count = lax.axis_size("seq")
    return lax.ppermute(value, "seq", [(i, (i + 2) % count) for i in range(count)])


def next_section(value, chips_on):
    sections, count = lax.axis_size("section"), lax.axis_size("seq")
    pairs = [
        (s * count + i, (s + 1) % sections * count + (i + 2 * chips_on) % count)
        for s in range(sections)
        for i in range(count)
    ]
    return lax.ppermute(value, ("section", "seq"), pairs)


IN_VMEM = pl.BlockSpec(memory_space=pltpu.VMEM)
IN_SMEM = pl.BlockSpec(memory_space=pltpu.SMEM)
PARAMS = pltpu.CompilerParams(vmem_limit_bytes=16 * 1024 * 1024)


def after(values, *others):
    return lax.optimization_barrier((values, others))[0]


def chip_at(where, steps, chips):
    return lax.rem(where[0] + (chips - steps), chips)


def project_kernel(where, *refs, steps, chips):
    xs, refs = refs[: 2 * PIECES], refs[2 * PIECES :]
    weights, outs = refs[:2], refs[-2:]
    core = where[1]
    tokens, depth = xs[0].shape
    start = chip_at(where, steps, chips) * (2 * tokens)
    mine = pl.ds(pl.multiple_of(start + core * tokens, tokens), tokens)
    other = pl.ds(pl.multiple_of(start + (1 - core) * tokens, tokens), tokens)
    tall = [
        jnp.concatenate([xs[i][...], xs[PIECES + i][...]], axis=0) for i in range(PIECES)
    ]
    for weight, out in zip(weights, outs):
        total = None
        for i, x in enumerate(tall):
            part = jnp.dot(
                x, weight[i * depth : (i + 1) * depth, :], preferred_element_type=f32
            )
            total = part if total is None else total + part
        total = total.astype(bf16)
        out[mine, :] = total[:tokens]
        out[other, :] = total[tokens:]


def project(where, steps, chips, xs, weights, length, buffers):
    args = [where, *xs, *weights]
    in_specs = [IN_SMEM] + [IN_VMEM] * (len(args) - 1)
    aliases = {}
    if buffers is not None:
        aliases = {len(args): 0, len(args) + 1: 1}
        args += list(buffers)
        in_specs += [IN_VMEM] * 2
    width = weights[0].shape[0]
    columns = sum(weight.shape[1] for weight in weights)
    return pl.pallas_call(
        functools.partial(project_kernel, steps=steps, chips=chips),
        in_specs=in_specs,
        out_specs=[IN_VMEM] * 2,
        out_shape=[jax.ShapeDtypeStruct((length, weight.shape[1]), bf16) for weight in weights],
        input_output_aliases=aliases,
        compiler_params=PARAMS,
        cost_estimate=pl.CostEstimate(
            flops=2 * (length // chips) * width * columns,
            bytes_accessed=2 * width * columns,
            transcendentals=0,
        ),
        name="project",
    )(*args)


def ready_kernel(where, xz_ref, p_ref, out):
    del xz_ref, p_ref
    out[0] = where[0]
    out[1] = where[1]


def ready(where, xz_local, p_local):
    anywhere = pl.BlockSpec(memory_space=pl.ANY)
    return pl.pallas_call(
        ready_kernel,
        in_specs=[IN_SMEM, anywhere, anywhere],
        out_specs=IN_SMEM,
        out_shape=jax.ShapeDtypeStruct(where.shape, where.dtype),
        compiler_params=PARAMS,
        name="ready",
    )(where, xz_local, p_local)


def spread_of(chans):
    return (
        lax.broadcasted_iota(jnp.int32, (LANES, chans), 0)
        == lax.broadcasted_iota(jnp.int32, (LANES, chans), 1) // HEAD_DIM
    )


def tables_kernel(
    where, conv_w, conv_b, step_b, decay, skip_w, norm_g,
    taps, offset, bias, rate, skip, gain,
):
    chans = gain.shape[1]
    heads = chans // HEAD_DIM
    member = where[0] * 2 + where[1]
    first = member * heads
    group = first // (HEADS // GROUPS)
    odd = lax.rem(group, 2) == 1
    own = pl.ds(pl.multiple_of(member * chans, LANES), chans)
    inner = HEADS * HEAD_DIM
    for table, out in ((conv_w, taps), (conv_b, offset)):
        out[:, :chans] = table[:, own]
        b_at = pl.multiple_of(inner + group // 2 * LANES, LANES)
        c_at = pl.multiple_of(inner + GROUPS * STATE + group // 2 * LANES, LANES)
        count = table.shape[0]
        rows = []
        for k in range(count):
            b = jnp.broadcast_to(table[k : k + 1, pl.ds(b_at, LANES)], (8, LANES))
            c = jnp.broadcast_to(table[k : k + 1, pl.ds(c_at, LANES)], (8, LANES))
            b = jnp.where(odd, pltpu.roll(b, STATE, 1), b)
            c = jnp.where(odd, c, pltpu.roll(c, STATE, 1))
            lane = lax.broadcasted_iota(jnp.int32, (8, LANES), 1)
            rows.append(jnp.where(lane < STATE, b, c)[0:1])
        for k in range(count):
            out[k : k + 1, chans:] = rows[k]
    back = lax.rem(HEADS - first, HEADS)

    def own_heads(table):
        return pltpu.roll(jnp.broadcast_to(table[...], (8, LANES)), back, 1)

    bias[...] = own_heads(step_b)[0:1]
    rate[...] = -jnp.exp(own_heads(decay)[0:1])
    skip[...] = jnp.dot(
        own_heads(skip_w),
        spread_of(chans).astype(f32),
        precision=lax.Precision.HIGHEST,
        preferred_element_type=f32,
    )[0:1]
    gain[...] = norm_g[:, own]


def tables_of(where, params, chans):
    shapes = (
        (CONV, chans + 2 * STATE), (1, chans + 2 * STATE), (1, LANES), (1, LANES), (1, chans),
        (1, chans),
    )
    return pl.pallas_call(
        tables_kernel,
        in_specs=[IN_SMEM] + [IN_VMEM] * len(params),
        out_specs=[IN_VMEM] * len(shapes),
        out_shape=[jax.ShapeDtypeStruct(shape, f32) for shape in shapes],
        compiler_params=PARAMS,
        name="tables",
    )(where, *params)


def silu(value):
    return value / (1.0 + jnp.exp(-value))


def split_terms(value, terms):
    parts = []
    for _ in range(terms - 1):
        parts.append(value.astype(bf16))
        value = value - parts[-1].astype(f32)
    return parts + [value.astype(bf16)]


def mix_kernel(
    where, xz_ref, p_ref, taps_ref, offset_ref, bias_ref, rate_ref, skip_ref, gain_ref,
    mine_ref, theirs_ref, mine_squares, theirs_squares,
    padded_ref, state_ref, gated_ref, squares_ref,
):
    chans = mine_ref.shape[1]
    heads = chans // HEAD_DIM
    lead = 8
    rows = pl.ds(pl.multiple_of(pl.program_id(0) * BLOCK, BLOCK), BLOCK)

    @pl.when(pl.program_id(0) == 0)
    def _():
        padded_ref[0:lead, :] = jnp.zeros((lead, padded_ref.shape[1]), f32)
        state_ref[...] = jnp.zeros_like(state_ref)

    padded_ref[lead : lead + BLOCK, 0:chans] = xz_ref[rows, chans:].astype(f32)
    padded_ref[lead : lead + BLOCK, chans:] = p_ref[rows, 0 : 2 * STATE].astype(f32)
    total = offset_ref[0:1, :]
    for k in range(CONV):
        start = lead - (CONV - 1) + k
        total = total + taps_ref[k : k + 1, :] * padded_ref[start : start + BLOCK, :]
    padded_ref[0:lead, :] = padded_ref[BLOCK : BLOCK + lead, :]
    convolved = silu(total).astype(bf16)
    x = convolved[:, :chans]
    bc = convolved[:, chans:]
    b = bc[:, :STATE]
    c = bc[:, STATE:]

    step = jax.nn.softplus(p_ref[rows, 2 * STATE :].astype(f32) + bias_ref[0:1, :])
    decay = rate_ref[0:1, :] * step
    row = lax.broadcasted_iota(jnp.int32, (BLOCK, BLOCK), 0)
    col = lax.broadcasted_iota(jnp.int32, (BLOCK, BLOCK), 1)
    lower = row >= col
    terms = split_terms(decay, 3)
    cumulus = jnp.dot(
        jnp.concatenate([lower.astype(bf16)] * len(terms), axis=1),
        jnp.concatenate(terms, axis=0),
        preferred_element_type=f32,
    )
    block_total = cumulus[BLOCK - 1 : BLOCK, :]
    cumulus_t = cumulus.T
    step_t = step.T
    scores = lax.dot_general(c, b, (((1,), (1,)), ((), ())), preferred_element_type=f32)
    spread = spread_of(chans).astype(bf16)
    spread = jnp.concatenate([spread, spread], axis=0)

    def per_channel(table):
        return jnp.dot(
            jnp.concatenate(split_terms(table, 2), axis=1), spread, preferred_element_type=f32
        )

    grown = per_channel(jnp.exp(cumulus))
    kept = per_channel(jnp.exp(block_total - cumulus) * step)
    x_wide = x.astype(f32)
    weighted = (x_wide * kept).astype(bf16)
    entering = state_ref[...].astype(bf16)
    carried = jnp.dot(c, entering, preferred_element_type=f32) * grown
    block_state = lax.dot_general(
        b, weighted, (((0,), (0,)), ((), ())), preferred_element_type=f32
    )
    state_ref[...] = grown[BLOCK - 1 : BLOCK, :] * state_ref[...] + block_state

    lane_head = lax.broadcasted_iota(jnp.int32, (BLOCK, LANES), 1) // HEAD_DIM
    squares = jnp.zeros((BLOCK, 1), f32)
    for quad in range(heads // QUAD):
        lanes = slice(quad * LANES, (quad + 1) * LANES)
        x_quad = x[:, lanes]
        left, right = [], []
        for j in range(QUAD):
            h = quad * QUAD + j
            gap = jnp.where(lower, cumulus[:, h : h + 1] - cumulus_t[h : h + 1, :], -1e30)
            left.append((scores * jnp.exp(gap) * step_t[h : h + 1, :]).astype(bf16))
            right.append(jnp.where(lane_head == j, x_quad, jnp.zeros_like(x_quad)))
        diagonal = jnp.dot(
            jnp.concatenate(left, axis=1),
            jnp.concatenate(right, axis=0),
            preferred_element_type=f32,
        )
        mixed = diagonal + carried[:, lanes] + skip_ref[0:1, lanes] * x_wide[:, lanes]
        gated = mixed * silu(xz_ref[rows, lanes].astype(f32))
        squares = squares + jnp.sum(gated * gated, axis=1, keepdims=True)
        gated_ref[:, lanes] = (gated * gain_ref[0:1, lanes]).astype(bf16)
    squares_ref[...] = jnp.broadcast_to(squares, (BLOCK, LANES))
    part = BLOCK // 2
    core = where[1]
    to = pl.ds(pl.multiple_of(pl.program_id(0) * part, part), part)
    near = pl.ds(pl.multiple_of(core * part, part), part)
    far = pl.ds(pl.multiple_of((1 - core) * part, part), part)
    mine_ref[to, :] = gated_ref[near, :]
    theirs_ref[to, :] = gated_ref[far, :]
    mine_squares[to, :] = squares_ref[near, :]
    theirs_squares[to, :] = squares_ref[far, :]


def mix(where, xz, p, tables):
    length, both = xz.shape
    chans = both // 2
    n_p = p.shape[1]
    return pl.pallas_call(
        mix_kernel,
        grid=(length // BLOCK,),
        in_specs=[IN_SMEM] + [IN_VMEM] * (2 + len(tables)),
        out_specs=[IN_VMEM] * 4,
        compiler_params=PARAMS,
        out_shape=[jax.ShapeDtypeStruct((length // 2, chans), bf16)] * 2
        + [jax.ShapeDtypeStruct((length // 2, LANES), f32)] * 2,
        scratch_shapes=[
            pltpu.VMEM((BLOCK + 8, chans + 2 * STATE), f32),
            pltpu.VMEM((STATE, chans), f32),
            pltpu.VMEM((BLOCK, chans), bf16),
            pltpu.VMEM((BLOCK, LANES), f32),
        ],
        cost_estimate=pl.CostEstimate(
            flops=2 * length * chans * BLOCK * 8,
            bytes_accessed=2 * length * (both + chans + n_p),
            transcendentals=length * chans * 4,
        ),
        name="mix",
    )(where, xz, p, *tables)


def out_kernel(where, g_mine, g_other, w_mine, w_other, *refs, steps, chips, first, count, scale):
    squares, outs = refs[:-count], refs[-count:]
    rows, tile = outs[0].shape
    at = pl.ds(pl.multiple_of(chip_at(where, steps, chips) * rows, rows), rows)
    total = squares[0][at, 0:1]
    for more in squares[1:]:
        total = total + more[at, 0:1]
    rate = lax.rsqrt(total * scale + 1e-05)
    for i, out in enumerate(outs):
        cols = slice((first + i) * tile, (first + i + 1) * tile)
        part = jnp.dot(g_mine[at, :], w_mine[:, cols], preferred_element_type=f32)
        part = part + jnp.dot(g_other[at, :], w_other[:, cols], preferred_element_type=f32)
        out[...] = (part * rate).astype(out.dtype)


def out_project(where, steps, chips, gated, weights, squares, pieces, dtype):
    chans, cols = weights[0].shape
    rows = gated[0].shape[0] // chips
    first, count = pieces
    args = [where, *gated, *weights, *squares]
    return pl.pallas_call(
        functools.partial(
            out_kernel,
            steps=steps,
            chips=chips,
            first=first,
            count=count,
            scale=GROUPS / (HEADS * HEAD_DIM),
        ),
        in_specs=[IN_SMEM] + [IN_VMEM] * (len(args) - 1),
        out_specs=[IN_VMEM] * count,
        out_shape=[jax.ShapeDtypeStruct((rows, cols // PIECES), dtype)] * count,
        compiler_params=PARAMS,
        cost_estimate=pl.CostEstimate(
            flops=4 * rows * chans * cols * count // PIECES,
            bytes_accessed=4 * chans * cols * count // PIECES,
            transcendentals=0,
        ),
        name="out_project",
    )(*args)


def on_device(
    inflow,
    fresh,
    proj_weight,
    xz_weight,
    conv_weight,
    conv_bias,
    step_bias,
    decay_log,
    skip_weight,
    norm_gain,
    out_weight,
):
    members = lax.axis_size("seq")
    sections = lax.axis_size("section")
    position = lax.axis_index("section")
    member = lax.axis_index("seq")
    chips = members // 2
    tokens, width = inflow.shape[1], inflow.shape[2]
    assert 2 * tokens == BLOCK
    length = tokens * members
    piece = width // PIECES
    heads_dev = HEADS // members
    chan_dev = heads_dev * HEAD_DIM
    bc_width = GROUPS * STATE
    group_members = members // GROUPS
    head_start = member * heads_dev
    group_index = head_start // (HEADS // GROUPS)
    where = jnp.stack([member // 2, member % 2]).astype(jnp.int32)

    def in_pieces(shard):
        return [shard[:, i * piece : (i + 1) * piece] for i in range(PIECES)]

    entering = in_pieces(inflow[0])
    arriving = [chip_ring(x) for x in entering]

    xz_local = xz_weight[0].reshape(width, 2 * chan_dev)
    column = lax.broadcasted_iota(jnp.int32, (proj_weight.shape[2], 2 * LANES), 1)
    source = jnp.where(
        column < STATE,
        group_index * STATE + column,
        jnp.where(
            column < 2 * STATE,
            bc_width + group_index * STATE + column - STATE,
            2 * bc_width + head_start + column - 2 * STATE,
        ),
    )
    chosen = (lax.broadcasted_iota(jnp.int32, column.shape, 0) == source) & (
        column < 2 * STATE + heads_dev
    )
    p_local = jnp.dot(
        proj_weight[0], chosen.astype(bf16), preferred_element_type=f32
    ).astype(bf16)
    where_ready = ready(where, xz_local, p_local)
    tables = tables_of(
        where, (conv_weight[0], conv_bias, step_bias, decay_log, skip_weight, norm_gain), chan_dev
    )
    out_weights = (out_weight[0], swapped(out_weight[0], 1))

    def layer(held, arriving):
        buffers = None
        for step in range(chips):
            if step == 1:
                held = arriving
            elif step > 1:
                held = [chip_ring(x) for x in held]
            other = [swapped(part, 1) for part in held]
            buffers = project(
                where_ready, step, chips, held + other, (xz_local, p_local), length, buffers
            )
        near, far, near_squares, far_squares = mix(where, *buffers, tables)
        gated = (near, swapped(far, 1))
        squares = []
        for mask in range(0, group_members, 2):
            squares.append(swapped(near_squares, mask) if mask else near_squares)
            squares.append(swapped(far_squares, mask ^ 1))
        running = None
        for step in range(1, chips + 1):
            calls = [(i, 1) for i in range(PIECES)] if step == 1 else [(0, PIECES)]
            parts = []
            for call in calls:
                parts += out_project(
                    where, step, chips, gated, out_weights, squares, call,
                    bf16 if step == 1 else f32,
                )
            if running is not None:
                parts = [part + came.astype(f32) for part, came in zip(parts, running)]
            if step < chips:
                running = [chip_ring(part.astype(bf16)) for part in parts]
        return parts

    first = layer(entering, arriving)
    leaving = [
        jnp.where(position == sections - 1, new, part.astype(bf16))
        for new, part in zip(in_pieces(fresh[0]), first)
    ]
    ahead = [next_section(x, 1) for x in leaving]
    level = [next_section(x, 0) for x in after(leaving, ahead)]
    second = layer(level, ahead)
    return jnp.stack([jnp.concatenate(first, axis=1), jnp.concatenate(second, axis=1)])[None]


def solution(mesh):
    placed = (
        P("section", "seq", None),
        P(None, "seq", None),
        P("section", None, None),
        P("section", None, None, "seq"),
        P("section", None, None),
        P("section", None),
        P("section", None),
        P("section", None),
        P("section", None),
        P("section", None),
        P("section", "seq", None),
    )

    return jax.shard_map(
        on_device,
        mesh=mesh,
        in_specs=placed,
        out_specs=P("section", None, "seq", None),
        check_vma=False,
    )
```

```python
import functools

import jax
import jax.numpy as jnp
from jax import lax
from jax.experimental import pallas as pl
from jax.experimental.pallas import tpu as pltpu
from jax.sharding import PartitionSpec as P


HEADS = 128
HEAD_DIM = 32
STATE = 64
GROUPS = 4
CONV = 4
BLOCK = 128
LANES = 128
PIECES = 2
QUAD = LANES // HEAD_DIM


bf16 = jnp.bfloat16
f32 = jnp.float32


def swapped(value, bit):
    count = lax.axis_size("seq")
    return lax.ppermute(value, "seq", [(i, i ^ bit) for i in range(count)])


def chip_ring(value):
    count = lax.axis_size("seq")
    return lax.ppermute(value, "seq", [(i, (i + 2) % count) for i in range(count)])


def next_section(value, chips_on):
    sections, count = lax.axis_size("section"), lax.axis_size("seq")
    pairs = [
        (s * count + i, (s + 1) % sections * count + (i + 2 * chips_on) % count)
        for s in range(sections)
        for i in range(count)
    ]
    return lax.ppermute(value, ("section", "seq"), pairs)


IN_VMEM = pl.BlockSpec(memory_space=pltpu.VMEM)
IN_SMEM = pl.BlockSpec(memory_space=pltpu.SMEM)
PARAMS = pltpu.CompilerParams(vmem_limit_bytes=16 * 1024 * 1024)


def after(values, *others):
    return lax.optimization_barrier((values, others))[0]


def chip_at(where, steps, chips):
    return lax.rem(where[0] + (chips - steps), chips)


def project_kernel(where, *refs, steps, chips):
    xs, refs = refs[: 2 * PIECES], refs[2 * PIECES :]
    xz_parts, p_weight, outs = refs[:PIECES], refs[PIECES], refs[-2:]
    core = where[1]
    tokens, depth = xs[0].shape
    start = chip_at(where, steps, chips) * (2 * tokens)
    mine = pl.ds(pl.multiple_of(start + core * tokens, tokens), tokens)
    other = pl.ds(pl.multiple_of(start + (1 - core) * tokens, tokens), tokens)
    tall = [
        jnp.concatenate([xs[i][...], xs[PIECES + i][...]], axis=0) for i in range(PIECES)
    ]
    p_parts = [p_weight.at[i * depth : (i + 1) * depth, :] for i in range(PIECES)]
    for weights, out in zip((xz_parts, p_parts), outs):
        total = None
        for x, weight in zip(tall, weights):
            part = jnp.dot(x, weight[...], preferred_element_type=f32)
            total = part if total is None else total + part
        total = total.astype(bf16)
        out[mine, :] = total[:tokens]
        out[other, :] = total[tokens:]


def project(where, steps, chips, xs, weights, length, buffers):
    args = [where, *xs, *weights]
    in_specs = [IN_SMEM] + [IN_VMEM] * (len(args) - 1)
    aliases = {}
    if buffers is not None:
        aliases = {len(args): 0, len(args) + 1: 1}
        args += list(buffers)
        in_specs += [IN_VMEM] * 2
    width = weights[-1].shape[0]
    n_out = [weights[0].shape[1], weights[-1].shape[1]]
    columns = sum(n_out)
    return pl.pallas_call(
        functools.partial(project_kernel, steps=steps, chips=chips),
        in_specs=in_specs,
        out_specs=[IN_VMEM] * 2,
        out_shape=[jax.ShapeDtypeStruct((length, n), bf16) for n in n_out],
        input_output_aliases=aliases,
        compiler_params=PARAMS,
        cost_estimate=pl.CostEstimate(
            flops=2 * (length // chips) * width * columns,
            bytes_accessed=2 * width * columns,
            transcendentals=0,
        ),
        name="project",
    )(*args)


def ready_kernel(where, weight, out):
    del weight
    out[0] = where[0]
    out[1] = where[1]


def ready(where, weight):
    return pl.pallas_call(
        ready_kernel,
        in_specs=[IN_SMEM, pl.BlockSpec(memory_space=pl.ANY)],
        out_specs=IN_SMEM,
        out_shape=jax.ShapeDtypeStruct(where.shape, where.dtype),
        compiler_params=PARAMS,
        name="ready",
    )(where, weight)


def stage_kernel(upper, lower, out, semaphores):
    rows = upper.shape[0]
    copies = [
        pltpu.make_async_copy(part, out.at[i * rows : (i + 1) * rows, :], semaphores.at[i])
        for i, part in enumerate((upper, lower))
    ]
    for copy in copies:
        copy.start()
    for copy in copies:
        copy.wait()


def stage(upper, lower):
    rows, cols = upper.shape
    return pl.pallas_call(
        stage_kernel,
        in_specs=[pl.BlockSpec(memory_space=pl.ANY)] * 2,
        out_specs=IN_VMEM,
        out_shape=jax.ShapeDtypeStruct((2 * rows, cols), upper.dtype),
        scratch_shapes=[pltpu.SemaphoreType.DMA((2,))],
        compiler_params=PARAMS,
        cost_estimate=pl.CostEstimate(
            flops=0, bytes_accessed=8 * rows * cols, transcendentals=0
        ),
        name="stage",
    )(upper, lower)


def spread_of(chans):
    return (
        lax.broadcasted_iota(jnp.int32, (LANES, chans), 0)
        == lax.broadcasted_iota(jnp.int32, (LANES, chans), 1) // HEAD_DIM
    )


def tables_kernel(
    where, conv_w, conv_b, step_b, decay, skip_w, norm_g,
    taps, offset, bias, rate, skip, gain,
):
    chans = gain.shape[1]
    heads = chans // HEAD_DIM
    member = where[0] * 2 + where[1]
    first = member * heads
    group = first // (HEADS // GROUPS)
    odd = lax.rem(group, 2) == 1
    own = pl.ds(pl.multiple_of(member * chans, LANES), chans)
    inner = HEADS * HEAD_DIM
    for table, out in ((conv_w, taps), (conv_b, offset)):
        out[:, :chans] = table[:, own]
        b_at = pl.multiple_of(inner + group // 2 * LANES, LANES)
        c_at = pl.multiple_of(inner + GROUPS * STATE + group // 2 * LANES, LANES)
        count = table.shape[0]
        rows = []
        for k in range(count):
            b = jnp.broadcast_to(table[k : k + 1, pl.ds(b_at, LANES)], (8, LANES))
            c = jnp.broadcast_to(table[k : k + 1, pl.ds(c_at, LANES)], (8, LANES))
            b = jnp.where(odd, pltpu.roll(b, STATE, 1), b)
            c = jnp.where(odd, c, pltpu.roll(c, STATE, 1))
            lane = lax.broadcasted_iota(jnp.int32, (8, LANES), 1)
            rows.append(jnp.where(lane < STATE, b, c)[0:1])
        for k in range(count):
            out[k : k + 1, chans:] = rows[k]
    back = lax.rem(HEADS - first, HEADS)

    def own_heads(table):
        return pltpu.roll(jnp.broadcast_to(table[...], (8, LANES)), back, 1)

    bias[...] = own_heads(step_b)[0:1]
    rate[...] = -jnp.exp(own_heads(decay)[0:1])
    skip[...] = jnp.dot(
        own_heads(skip_w),
        spread_of(chans).astype(f32),
        precision=lax.Precision.HIGHEST,
        preferred_element_type=f32,
    )[0:1]
    gain[...] = norm_g[:, own]


def tables_of(where, params, chans):
    shapes = (
        (CONV, chans + 2 * STATE), (1, chans + 2 * STATE), (1, LANES), (1, LANES), (1, chans),
        (1, chans),
    )
    return pl.pallas_call(
        tables_kernel,
        in_specs=[IN_SMEM] + [IN_VMEM] * len(params),
        out_specs=[IN_VMEM] * len(shapes),
        out_shape=[jax.ShapeDtypeStruct(shape, f32) for shape in shapes],
        compiler_params=PARAMS,
        name="tables",
    )(where, *params)


def silu(value):
    return value / (1.0 + jnp.exp(-value))


def split_terms(value, terms):
    parts = []
    for _ in range(terms - 1):
        parts.append(value.astype(bf16))
        value = value - parts[-1].astype(f32)
    return parts + [value.astype(bf16)]


def mix_kernel(
    where, xz_ref, p_ref, taps_ref, offset_ref, bias_ref, rate_ref, skip_ref, gain_ref,
    mine_ref, theirs_ref, mine_squares, theirs_squares,
    padded_ref, state_ref, gated_ref, squares_ref,
):
    chans = mine_ref.shape[1]
    heads = chans // HEAD_DIM
    lead = 8
    rows = pl.ds(pl.multiple_of(pl.program_id(0) * BLOCK, BLOCK), BLOCK)

    @pl.when(pl.program_id(0) == 0)
    def _():
        padded_ref[0:lead, :] = jnp.zeros((lead, padded_ref.shape[1]), f32)
        state_ref[...] = jnp.zeros_like(state_ref)

    padded_ref[lead : lead + BLOCK, 0:chans] = xz_ref[rows, chans:].astype(f32)
    padded_ref[lead : lead + BLOCK, chans:] = p_ref[rows, 0 : 2 * STATE].astype(f32)
    total = offset_ref[0:1, :]
    for k in range(CONV):
        start = lead - (CONV - 1) + k
        total = total + taps_ref[k : k + 1, :] * padded_ref[start : start + BLOCK, :]
    padded_ref[0:lead, :] = padded_ref[BLOCK : BLOCK + lead, :]
    convolved = silu(total).astype(bf16)
    x = convolved[:, :chans]
    bc = convolved[:, chans:]
    b = bc[:, :STATE]
    c = bc[:, STATE:]

    step = jax.nn.softplus(p_ref[rows, 2 * STATE :].astype(f32) + bias_ref[0:1, :])
    decay = rate_ref[0:1, :] * step
    row = lax.broadcasted_iota(jnp.int32, (BLOCK, BLOCK), 0)
    col = lax.broadcasted_iota(jnp.int32, (BLOCK, BLOCK), 1)
    lower = row >= col
    terms = split_terms(decay, 3)
    cumulus = jnp.dot(
        jnp.concatenate([lower.astype(bf16)] * len(terms), axis=1),
        jnp.concatenate(terms, axis=0),
        preferred_element_type=f32,
    )
    block_total = cumulus[BLOCK - 1 : BLOCK, :]
    cumulus_t = cumulus.T
    step_t = step.T
    scores = lax.dot_general(c, b, (((1,), (1,)), ((), ())), preferred_element_type=f32)
    spread = spread_of(chans).astype(bf16)
    spread = jnp.concatenate([spread, spread], axis=0)

    def per_channel(table):
        return jnp.dot(
            jnp.concatenate(split_terms(table, 2), axis=1), spread, preferred_element_type=f32
        )

    grown = per_channel(jnp.exp(cumulus))
    kept = per_channel(jnp.exp(block_total - cumulus) * step)
    x_wide = x.astype(f32)
    weighted = (x_wide * kept).astype(bf16)
    entering = state_ref[...].astype(bf16)
    carried = jnp.dot(c, entering, preferred_element_type=f32) * grown
    block_state = lax.dot_general(
        b, weighted, (((0,), (0,)), ((), ())), preferred_element_type=f32
    )
    state_ref[...] = grown[BLOCK - 1 : BLOCK, :] * state_ref[...] + block_state

    lane_head = lax.broadcasted_iota(jnp.int32, (BLOCK, LANES), 1) // HEAD_DIM
    squares = jnp.zeros((BLOCK, 1), f32)
    for quad in range(heads // QUAD):
        lanes = slice(quad * LANES, (quad + 1) * LANES)
        x_quad = x[:, lanes]
        left, right = [], []
        for j in range(QUAD):
            h = quad * QUAD + j
            gap = jnp.where(lower, cumulus[:, h : h + 1] - cumulus_t[h : h + 1, :], -1e30)
            left.append((scores * jnp.exp(gap) * step_t[h : h + 1, :]).astype(bf16))
            right.append(jnp.where(lane_head == j, x_quad, jnp.zeros_like(x_quad)))
        diagonal = jnp.dot(
            jnp.concatenate(left, axis=1),
            jnp.concatenate(right, axis=0),
            preferred_element_type=f32,
        )
        mixed = diagonal + carried[:, lanes] + skip_ref[0:1, lanes] * x_wide[:, lanes]
        gated = mixed * silu(xz_ref[rows, lanes].astype(f32))
        squares = squares + jnp.sum(gated * gated, axis=1, keepdims=True)
        gated_ref[:, lanes] = (gated * gain_ref[0:1, lanes]).astype(bf16)
    squares_ref[...] = jnp.broadcast_to(squares, (BLOCK, LANES))
    part = BLOCK // 2
    core = where[1]
    to = pl.ds(pl.multiple_of(pl.program_id(0) * part, part), part)
    near = pl.ds(pl.multiple_of(core * part, part), part)
    far = pl.ds(pl.multiple_of((1 - core) * part, part), part)
    mine_ref[to, :] = gated_ref[near, :]
    theirs_ref[to, :] = gated_ref[far, :]
    mine_squares[to, :] = squares_ref[near, :]
    theirs_squares[to, :] = squares_ref[far, :]


def mix(where, xz, p, tables):
    length, both = xz.shape
    chans = both // 2
    n_p = p.shape[1]
    return pl.pallas_call(
        mix_kernel,
        grid=(length // BLOCK,),
        in_specs=[IN_SMEM] + [IN_VMEM] * (2 + len(tables)),
        out_specs=[IN_VMEM] * 4,
        compiler_params=PARAMS,
        out_shape=[jax.ShapeDtypeStruct((length // 2, chans), bf16)] * 2
        + [jax.ShapeDtypeStruct((length // 2, LANES), f32)] * 2,
        scratch_shapes=[
            pltpu.VMEM((BLOCK + 8, chans + 2 * STATE), f32),
            pltpu.VMEM((STATE, chans), f32),
            pltpu.VMEM((BLOCK, chans), bf16),
            pltpu.VMEM((BLOCK, LANES), f32),
        ],
        cost_estimate=pl.CostEstimate(
            flops=2 * length * chans * BLOCK * 8,
            bytes_accessed=2 * length * (both + chans + n_p),
            transcendentals=length * chans * 4,
        ),
        name="mix",
    )(where, xz, p, *tables)


def out_kernel(where, g_mine, g_other, weight, *refs, steps, chips, first, count, scale):
    squares, outs = refs[:-count], refs[-count:]
    rows, tile = outs[0].shape
    at = pl.ds(pl.multiple_of(chip_at(where, steps, chips) * rows, rows), rows)
    total = squares[0][at, 0:1]
    for more in squares[1:]:
        total = total + more[at, 0:1]
    rate = lax.rsqrt(total * scale + 1e-05)
    both = jnp.concatenate([g_mine[at, :], g_other[at, :]], axis=1)
    for i, out in enumerate(outs):
        cols = slice((first + i) * tile, (first + i + 1) * tile)
        part = jnp.dot(both, weight[:, cols], preferred_element_type=f32)
        out[...] = (part * rate).astype(out.dtype)


def out_project(where, steps, chips, gated, weight, squares, pieces, dtype):
    chans, cols = weight.shape
    rows = gated[0].shape[0] // chips
    first, count = pieces
    args = [where, *gated, weight, *squares]
    return pl.pallas_call(
        functools.partial(
            out_kernel,
            steps=steps,
            chips=chips,
            first=first,
            count=count,
            scale=GROUPS / (HEADS * HEAD_DIM),
        ),
        in_specs=[IN_SMEM] + [IN_VMEM] * (len(args) - 1),
        out_specs=[IN_VMEM] * count,
        out_shape=[jax.ShapeDtypeStruct((rows, cols // PIECES), dtype)] * count,
        compiler_params=PARAMS,
        cost_estimate=pl.CostEstimate(
            flops=2 * rows * chans * cols * count // PIECES,
            bytes_accessed=2 * chans * cols * count // PIECES,
            transcendentals=0,
        ),
        name="out_project",
    )(*args)


def on_device(
    inflow,
    fresh,
    proj_weight,
    xz_weight,
    conv_weight,
    conv_bias,
    step_bias,
    decay_log,
    skip_weight,
    norm_gain,
    out_weight,
):
    members = lax.axis_size("seq")
    sections = lax.axis_size("section")
    position = lax.axis_index("section")
    member = lax.axis_index("seq")
    chips = members // 2
    tokens, width = inflow.shape[1], inflow.shape[2]
    assert 2 * tokens == BLOCK
    length = tokens * members
    piece = width // PIECES
    heads_dev = HEADS // members
    chan_dev = heads_dev * HEAD_DIM
    bc_width = GROUPS * STATE
    group_members = members // GROUPS
    head_start = member * heads_dev
    group_index = head_start // (HEADS // GROUPS)
    where = jnp.stack([member // 2, member % 2]).astype(jnp.int32)

    def in_pieces(shard):
        return [shard[:, i * piece : (i + 1) * piece] for i in range(PIECES)]

    entering = in_pieces(inflow[0])
    arriving = [chip_ring(x) for x in entering]

    def regrouped(weight, i):
        rows = slice(i * piece, (i + 1) * piece)
        return weight[0, rows].reshape(piece, 2 * chan_dev)

    xz_parts = [regrouped(xz_weight, 0)]
    column = lax.broadcasted_iota(jnp.int32, (proj_weight.shape[2], 2 * LANES), 1)
    source = jnp.where(
        column < STATE,
        group_index * STATE + column,
        jnp.where(
            column < 2 * STATE,
            bc_width + group_index * STATE + column - STATE,
            2 * bc_width + head_start + column - 2 * STATE,
        ),
    )
    chosen = (lax.broadcasted_iota(jnp.int32, column.shape, 0) == source) & (
        column < 2 * STATE + heads_dev
    )
    where_ready = ready(where, xz_parts[0])
    p_local = jnp.dot(
        after(proj_weight[0], where_ready), chosen.astype(bf16), preferred_element_type=f32
    ).astype(bf16)
    xz_parts += [regrouped(after(xz_weight, where_ready), i) for i in range(1, PIECES)]
    tables = tables_of(
        where_ready, (conv_weight[0], conv_bias, step_bias, decay_log, skip_weight, norm_gain), chan_dev
    )
    out_swapped = swapped(out_weight[0], 1)

    def layer(held, arriving, staged=None):
        buffers = None
        indices = where_ready
        pausing = staged is not None
        for step in range(chips):
            if step == chips - 1 and staged is None:
                staged = stage(after(out_weight[0], buffers), out_swapped)
            if step == 1:
                held = arriving
            elif step > 1:
                if pausing:
                    indices = ready(indices, held[0])
                held = [chip_ring(x) for x in held]
            other = [swapped(part, 1) for part in held]
            buffers = project(
                indices, step, chips, held + other, (*xz_parts, p_local), length, buffers
            )
        near, far, near_squares, far_squares = mix(where, *buffers, tables)
        gated = (near, swapped(far, 1))
        squares = []
        for mask in range(0, group_members, 2):
            squares.append(swapped(near_squares, mask) if mask else near_squares)
            squares.append(swapped(far_squares, mask ^ 1))
        running = parts = None
        for step in range(1, chips + 1):
            gate = where if parts is None else after(where, parts)
            calls = [(i, 1) for i in range(PIECES)] if step == 1 else [(0, PIECES)]
            parts = []
            for call in calls:
                parts += out_project(
                    after(gate, parts) if parts else gate, step, chips, gated, staged, squares, call,
                    bf16 if step == 1 else f32,
                )
            if running is not None:
                sums = []
                for part, came in zip(parts, running):
                    came = after(came, sums) if sums else came
                    sums.append(part + came.astype(f32))
                parts = sums
            if step < chips:
                parts = [part.astype(bf16) for part in parts]
                running = [chip_ring(x) for x in parts]
        return parts, staged

    first, staged = layer(entering, arriving)
    leaving = []
    for i, new in enumerate(in_pieces(fresh[0])):
        if leaving:
            first[i] = after(first[i], leaving)
        leaving.append(jnp.where(position == sections - 1, new, first[i].astype(bf16)))
    ahead = [next_section(x, 1) for x in leaving]
    level = [next_section(x, 0) for x in after(leaving, ahead)]
    second, _ = layer(level, ahead, staged)
    return jnp.stack([jnp.concatenate(first, axis=1), jnp.concatenate(second, axis=1)])[None]


def solution(mesh):
    placed = (
        P("section", "seq", None),
        P(None, "seq", None),
        P("section", None, None),
        P("section", None, None, "seq"),
        P("section", None, None),
        P("section", None),
        P("section", None),
        P("section", None),
        P("section", None),
        P("section", None),
        P("section", "seq", None),
    )

    return jax.shard_map(
        on_device,
        mesh=mesh,
        in_specs=placed,
        out_specs=P("section", None, "seq", None),
        check_vma=False,
    )
```

```python
import functools

import jax
import jax.numpy as jnp
from jax import lax
from jax.experimental import pallas as pl
from jax.experimental.pallas import tpu as pltpu
from jax.sharding import PartitionSpec as P


HEADS = 128
HEAD_DIM = 32
STATE = 64
GROUPS = 4
CONV = 4
BLOCK = 128
LANES = 128
PIECES = 2
QUAD = LANES // HEAD_DIM


bf16 = jnp.bfloat16
f32 = jnp.float32


def swapped(value, bit):
    count = lax.axis_size("seq")
    return lax.ppermute(value, "seq", [(i, i ^ bit) for i in range(count)])


def chip_ring(value):
    count = lax.axis_size("seq")
    return lax.ppermute(value, "seq", [(i, (i + 2) % count) for i in range(count)])


def next_section(value, chips_on):
    sections, count = lax.axis_size("section"), lax.axis_size("seq")
    pairs = [
        (s * count + i, (s + 1) % sections * count + (i + 2 * chips_on) % count)
        for s in range(sections)
        for i in range(count)
    ]
    return lax.ppermute(value, ("section", "seq"), pairs)


IN_VMEM = pl.BlockSpec(memory_space=pltpu.VMEM)
IN_SMEM = pl.BlockSpec(memory_space=pltpu.SMEM)
PARAMS = pltpu.CompilerParams(vmem_limit_bytes=16 * 1024 * 1024)


def after(values, *others):
    return lax.optimization_barrier((values, others))[0]


def chip_at(where, steps, chips):
    return lax.rem(where[0] + (chips - steps), chips)


def project_kernel(where, *refs, steps, chips):
    xs, refs = refs[: 2 * PIECES], refs[2 * PIECES :]
    xz_parts, p_weight, outs = refs[:PIECES], refs[PIECES], refs[-2:]
    core = where[1]
    tokens, depth = xs[0].shape
    start = chip_at(where, steps, chips) * (2 * tokens)
    mine = pl.ds(pl.multiple_of(start + core * tokens, tokens), tokens)
    other = pl.ds(pl.multiple_of(start + (1 - core) * tokens, tokens), tokens)
    tall = [
        jnp.concatenate([xs[i][...], xs[PIECES + i][...]], axis=0) for i in range(PIECES)
    ]
    p_parts = [p_weight.at[i * depth : (i + 1) * depth, :] for i in range(PIECES)]
    for weights, out in zip((xz_parts, p_parts), outs):
        total = None
        for x, weight in zip(tall, weights):
            part = jnp.dot(x, weight[...], preferred_element_type=f32)
            total = part if total is None else total + part
        total = total.astype(bf16)
        out[mine, :] = total[:tokens]
        out[other, :] = total[tokens:]


def project(where, steps, chips, xs, weights, length, buffers):
    args = [where, *xs, *weights]
    in_specs = [IN_SMEM] + [IN_VMEM] * (len(args) - 1)
    aliases = {}
    if buffers is not None:
        aliases = {len(args): 0, len(args) + 1: 1}
        args += list(buffers)
        in_specs += [IN_VMEM] * 2
    width = weights[-1].shape[0]
    n_out = [weights[0].shape[1], weights[-1].shape[1]]
    columns = sum(n_out)
    return pl.pallas_call(
        functools.partial(project_kernel, steps=steps, chips=chips),
        in_specs=in_specs,
        out_specs=[IN_VMEM] * 2,
        out_shape=[jax.ShapeDtypeStruct((length, n), bf16) for n in n_out],
        input_output_aliases=aliases,
        compiler_params=PARAMS,
        cost_estimate=pl.CostEstimate(
            flops=2 * (length // chips) * width * columns,
            bytes_accessed=2 * width * columns,
            transcendentals=0,
        ),
        name="project",
    )(*args)


def ready_kernel(where, weight, out):
    del weight
    out[0] = where[0]
    out[1] = where[1]


def ready(where, weight):
    return pl.pallas_call(
        ready_kernel,
        in_specs=[IN_SMEM, pl.BlockSpec(memory_space=pl.ANY)],
        out_specs=IN_SMEM,
        out_shape=jax.ShapeDtypeStruct(where.shape, where.dtype),
        compiler_params=PARAMS,
        name="ready",
    )(where, weight)


def stage_kernel(upper, lower, out, semaphores):
    rows = upper.shape[0]
    copies = [
        pltpu.make_async_copy(part, out.at[i * rows : (i + 1) * rows, :], semaphores.at[i])
        for i, part in enumerate((upper, lower))
    ]
    for copy in copies:
        copy.start()
    for copy in copies:
        copy.wait()


def stage(upper, lower):
    rows, cols = upper.shape
    return pl.pallas_call(
        stage_kernel,
        in_specs=[pl.BlockSpec(memory_space=pl.ANY)] * 2,
        out_specs=IN_VMEM,
        out_shape=jax.ShapeDtypeStruct((2 * rows, cols), upper.dtype),
        scratch_shapes=[pltpu.SemaphoreType.DMA((2,))],
        compiler_params=PARAMS,
        cost_estimate=pl.CostEstimate(
            flops=0, bytes_accessed=8 * rows * cols, transcendentals=0
        ),
        name="stage",
    )(upper, lower)


def spread_of(chans):
    return (
        lax.broadcasted_iota(jnp.int32, (LANES, chans), 0)
        == lax.broadcasted_iota(jnp.int32, (LANES, chans), 1) // HEAD_DIM
    )


def tables_kernel(
    where, conv_w, conv_b, step_b, decay, skip_w, norm_g,
    taps, offset, bias, rate, skip, gain,
):
    chans = gain.shape[1]
    heads = chans // HEAD_DIM
    member = where[0] * 2 + where[1]
    first = member * heads
    group = first // (HEADS // GROUPS)
    odd = lax.rem(group, 2) == 1
    own = pl.ds(pl.multiple_of(member * chans, LANES), chans)
    inner = HEADS * HEAD_DIM
    for table, out in ((conv_w, taps), (conv_b, offset)):
        out[:, :chans] = table[:, own]
        b_at = pl.multiple_of(inner + group // 2 * LANES, LANES)
        c_at = pl.multiple_of(inner + GROUPS * STATE + group // 2 * LANES, LANES)
        count = table.shape[0]
        rows = []
        for k in range(count):
            b = jnp.broadcast_to(table[k : k + 1, pl.ds(b_at, LANES)], (8, LANES))
            c = jnp.broadcast_to(table[k : k + 1, pl.ds(c_at, LANES)], (8, LANES))
            b = jnp.where(odd, pltpu.roll(b, STATE, 1), b)
            c = jnp.where(odd, c, pltpu.roll(c, STATE, 1))
            lane = lax.broadcasted_iota(jnp.int32, (8, LANES), 1)
            rows.append(jnp.where(lane < STATE, b, c)[0:1])
        for k in range(count):
            out[k : k + 1, chans:] = rows[k]
    back = lax.rem(HEADS - first, HEADS)

    def own_heads(table):
        return pltpu.roll(jnp.broadcast_to(table[...], (8, LANES)), back, 1)

    bias[...] = own_heads(step_b)[0:1]
    rate[...] = -jnp.exp(own_heads(decay)[0:1])
    skip[...] = jnp.dot(
        own_heads(skip_w),
        spread_of(chans).astype(f32),
        precision=lax.Precision.HIGHEST,
        preferred_element_type=f32,
    )[0:1]
    gain[...] = norm_g[:, own]


def tables_of(where, params, chans):
    shapes = (
        (CONV, chans + 2 * STATE), (1, chans + 2 * STATE), (1, LANES), (1, LANES), (1, chans),
        (1, chans),
    )
    return pl.pallas_call(
        tables_kernel,
        in_specs=[IN_SMEM] + [IN_VMEM] * len(params),
        out_specs=[IN_VMEM] * len(shapes),
        out_shape=[jax.ShapeDtypeStruct(shape, f32) for shape in shapes],
        compiler_params=PARAMS,
        name="tables",
    )(where, *params)


LOG2_E = 1.4426950408889634


def silu(value):
    half = 0.5 * value
    return half + half * jnp.tanh(half)


def split_terms(value, terms):
    parts = []
    for _ in range(terms - 1):
        parts.append(value.astype(bf16))
        value = value - parts[-1].astype(f32)
    return parts + [value.astype(bf16)]


def mix_kernel(
    where, xz_ref, p_ref, taps_ref, offset_ref, bias_ref, rate_ref, skip_ref, gain_ref,
    mine_ref, theirs_ref, mine_squares, theirs_squares,
    padded_ref, state_ref, gated_ref, squares_ref,
):
    chans = mine_ref.shape[1]
    heads = chans // HEAD_DIM
    lead = 8
    rows = pl.ds(pl.multiple_of(pl.program_id(0) * BLOCK, BLOCK), BLOCK)

    @pl.when(pl.program_id(0) == 0)
    def _():
        padded_ref[0:lead, :] = jnp.zeros((lead, padded_ref.shape[1]), f32)
        state_ref[...] = jnp.zeros_like(state_ref)

    padded_ref[lead : lead + BLOCK, 0:chans] = xz_ref[rows, chans:].astype(f32)
    padded_ref[lead : lead + BLOCK, chans:] = p_ref[rows, 0 : 2 * STATE].astype(f32)
    total = offset_ref[0:1, :]
    for k in range(CONV):
        start = lead - (CONV - 1) + k
        total = total + taps_ref[k : k + 1, :] * padded_ref[start : start + BLOCK, :]
    padded_ref[0:lead, :] = padded_ref[BLOCK : BLOCK + lead, :]
    convolved = silu(total).astype(bf16)
    x = convolved[:, :chans]
    bc = convolved[:, chans:]
    b = bc[:, :STATE]
    c = bc[:, STATE:]

    step = jax.nn.softplus(p_ref[rows, 2 * STATE :].astype(f32) + bias_ref[0:1, :])
    decay = rate_ref[0:1, :] * step
    row = lax.broadcasted_iota(jnp.int32, (BLOCK, BLOCK), 0)
    col = lax.broadcasted_iota(jnp.int32, (BLOCK, BLOCK), 1)
    lower = row >= col
    terms = split_terms(decay, 3)
    cumulus = jnp.dot(
        jnp.concatenate([lower.astype(bf16)] * len(terms), axis=1),
        jnp.concatenate(terms, axis=0),
        preferred_element_type=f32,
    )
    block_total = cumulus[BLOCK - 1 : BLOCK, :]
    scaled = cumulus * LOG2_E
    lowered_t = (scaled - jnp.log2(step)).T
    scores = lax.dot_general(c, b, (((1,), (1,)), ((), ())), preferred_element_type=f32)
    spread = spread_of(chans).astype(bf16)
    spread = jnp.concatenate([spread, spread], axis=0)

    def per_channel(table):
        return jnp.dot(
            jnp.concatenate(split_terms(table, 2), axis=1), spread, preferred_element_type=f32
        )

    grown = per_channel(jnp.exp(cumulus))
    kept = per_channel(jnp.exp(block_total - cumulus) * step)
    x_wide = x.astype(f32)
    weighted = (x_wide * kept).astype(bf16)
    entering = state_ref[...].astype(bf16)
    carried = jnp.dot(c, entering, preferred_element_type=f32) * grown
    block_state = lax.dot_general(
        b, weighted, (((0,), (0,)), ((), ())), preferred_element_type=f32
    )
    state_ref[...] = grown[BLOCK - 1 : BLOCK, :] * state_ref[...] + block_state

    lane_head = lax.broadcasted_iota(jnp.int32, (BLOCK, LANES), 1) // HEAD_DIM
    squares = jnp.zeros((BLOCK, 1), f32)
    for quad in range(heads // QUAD):
        lanes = slice(quad * LANES, (quad + 1) * LANES)
        x_quad = x[:, lanes]
        left, right = [], []
        for j in range(QUAD):
            h = quad * QUAD + j
            gap = jnp.where(lower, scaled[:, h : h + 1] - lowered_t[h : h + 1, :], -1e30)
            left.append((scores * jnp.exp2(gap)).astype(bf16))
            right.append(jnp.where(lane_head == j, x_quad, jnp.zeros_like(x_quad)))
        diagonal = jnp.dot(
            jnp.concatenate(left, axis=1),
            jnp.concatenate(right, axis=0),
            preferred_element_type=f32,
        )
        mixed = diagonal + carried[:, lanes] + skip_ref[0:1, lanes] * x_wide[:, lanes]
        gated = mixed * silu(xz_ref[rows, lanes].astype(f32))
        squares = squares + jnp.sum(gated * gated, axis=1, keepdims=True)
        gated_ref[:, lanes] = (gated * gain_ref[0:1, lanes]).astype(bf16)
    squares_ref[...] = jnp.broadcast_to(squares, (BLOCK, LANES))
    part = BLOCK // 2
    core = where[1]
    to = pl.ds(pl.multiple_of(pl.program_id(0) * part, part), part)
    near = pl.ds(pl.multiple_of(core * part, part), part)
    far = pl.ds(pl.multiple_of((1 - core) * part, part), part)
    mine_ref[to, :] = gated_ref[near, :]
    theirs_ref[to, :] = gated_ref[far, :]
    mine_squares[to, :] = squares_ref[near, :]
    theirs_squares[to, :] = squares_ref[far, :]


def mix(where, xz, p, tables):
    length, both = xz.shape
    chans = both // 2
    n_p = p.shape[1]
    return pl.pallas_call(
        mix_kernel,
        grid=(length // BLOCK,),
        in_specs=[IN_SMEM] + [IN_VMEM] * (2 + len(tables)),
        out_specs=[IN_VMEM] * 4,
        compiler_params=PARAMS,
        out_shape=[jax.ShapeDtypeStruct((length // 2, chans), bf16)] * 2
        + [jax.ShapeDtypeStruct((length // 2, LANES), f32)] * 2,
        scratch_shapes=[
            pltpu.VMEM((BLOCK + 8, chans + 2 * STATE), f32),
            pltpu.VMEM((STATE, chans), f32),
            pltpu.VMEM((BLOCK, chans), bf16),
            pltpu.VMEM((BLOCK, LANES), f32),
        ],
        cost_estimate=pl.CostEstimate(
            flops=2 * length * chans * BLOCK * 8,
            bytes_accessed=2 * length * (both + chans + n_p),
            transcendentals=length * chans * 4,
        ),
        name="mix",
    )(where, xz, p, *tables)


def out_kernel(where, g_mine, g_other, weight, *refs, steps, chips, first, count, scale):
    squares, outs = refs[:-count], refs[-count:]
    rows, tile = outs[0].shape
    at = pl.ds(pl.multiple_of(chip_at(where, steps, chips) * rows, rows), rows)
    total = squares[0][at, 0:1]
    for more in squares[1:]:
        total = total + more[at, 0:1]
    rate = lax.rsqrt(total * scale + 1e-05)
    both = jnp.concatenate([g_mine[at, :], g_other[at, :]], axis=1)
    for i, out in enumerate(outs):
        cols = slice((first + i) * tile, (first + i + 1) * tile)
        part = jnp.dot(both, weight[:, cols], preferred_element_type=f32)
        out[...] = (part * rate).astype(out.dtype)


def out_project(where, steps, chips, gated, weight, squares, pieces, dtype):
    chans, cols = weight.shape
    rows = gated[0].shape[0] // chips
    first, count = pieces
    args = [where, *gated, weight, *squares]
    return pl.pallas_call(
        functools.partial(
            out_kernel,
            steps=steps,
            chips=chips,
            first=first,
            count=count,
            scale=GROUPS / (HEADS * HEAD_DIM),
        ),
        in_specs=[IN_SMEM] + [IN_VMEM] * (len(args) - 1),
        out_specs=[IN_VMEM] * count,
        out_shape=[jax.ShapeDtypeStruct((rows, cols // PIECES), dtype)] * count,
        compiler_params=PARAMS,
        cost_estimate=pl.CostEstimate(
            flops=2 * rows * chans * cols * count // PIECES,
            bytes_accessed=2 * chans * cols * count // PIECES,
            transcendentals=0,
        ),
        name="out_project",
    )(*args)


def on_device(
    inflow,
    fresh,
    proj_weight,
    xz_weight,
    conv_weight,
    conv_bias,
    step_bias,
    decay_log,
    skip_weight,
    norm_gain,
    out_weight,
):
    members = lax.axis_size("seq")
    sections = lax.axis_size("section")
    position = lax.axis_index("section")
    member = lax.axis_index("seq")
    chips = members // 2
    tokens, width = inflow.shape[1], inflow.shape[2]
    assert 2 * tokens == BLOCK
    length = tokens * members
    piece = width // PIECES
    heads_dev = HEADS // members
    chan_dev = heads_dev * HEAD_DIM
    bc_width = GROUPS * STATE
    group_members = members // GROUPS
    head_start = member * heads_dev
    group_index = head_start // (HEADS // GROUPS)
    where = jnp.stack([member // 2, member % 2]).astype(jnp.int32)

    def in_pieces(shard):
        return [shard[:, i * piece : (i + 1) * piece] for i in range(PIECES)]

    entering = in_pieces(inflow[0])
    traded = [swapped(entering[0], 1)]
    arriving = []
    for i, x in enumerate(entering):
        x = after(x, traded) if i else x
        arriving.append(chip_ring(x))

    def regrouped(weight, i):
        rows = slice(i * piece, (i + 1) * piece)
        return weight[0, rows].reshape(piece, 2 * chan_dev)

    xz_parts = [regrouped(xz_weight, 0)]
    column = lax.broadcasted_iota(jnp.int32, (proj_weight.shape[2], 2 * LANES), 1)
    source = jnp.where(
        column < STATE,
        group_index * STATE + column,
        jnp.where(
            column < 2 * STATE,
            bc_width + group_index * STATE + column - STATE,
            2 * bc_width + head_start + column - 2 * STATE,
        ),
    )
    chosen = (lax.broadcasted_iota(jnp.int32, column.shape, 0) == source) & (
        column < 2 * STATE + heads_dev
    )
    where_ready = ready(where, xz_parts[0])
    p_local = jnp.dot(
        after(proj_weight[0], where_ready), chosen.astype(bf16), preferred_element_type=f32
    ).astype(bf16)
    xz_parts += [regrouped(after(xz_weight, where_ready), i) for i in range(1, PIECES)]
    tables = tables_of(
        where_ready, (conv_weight[0], conv_bias, step_bias, decay_log, skip_weight, norm_gain), chan_dev
    )
    out_swapped = swapped(out_weight[0], 1)

    def layer(held, arriving, where_ready, traded=(), staged=None):
        traded = list(traded)
        buffers = None
        indices = where_ready
        pausing = staged is not None
        for step in range(chips):
            if step == chips - 1 and staged is None:
                staged = stage(after(out_weight[0], buffers), out_swapped)
            if step == 1:
                held = arriving
            elif step > 1:
                if pausing:
                    indices = ready(indices, held[0])
                held = [chip_ring(x) for x in held]
            other = [swapped(part, 1) for part in held[len(traded) :]]
            other, traded = traded + other, []
            buffers = project(
                indices, step, chips, held + other, (*xz_parts, p_local), length, buffers
            )
        near, far, near_squares, far_squares = mix(where, *buffers, tables)
        gated = (near, swapped(far, 1))
        squares = []
        for mask in range(0, group_members, 2):
            squares.append(swapped(near_squares, mask) if mask else near_squares)
            squares.append(swapped(far_squares, mask ^ 1))
        running = parts = None
        for step in range(1, chips + 1):
            gate = where if parts is None else after(where, parts)
            calls = [(i, 1) for i in range(PIECES)] if step == 1 else [(0, PIECES)]
            parts = []
            for call in calls:
                parts += out_project(
                    after(gate, parts) if parts else gate, step, chips, gated, staged, squares, call,
                    bf16 if step == 1 else f32,
                )
            if running is not None:
                sums = []
                for part, came in zip(parts, running):
                    came = after(came, sums) if sums else came
                    sums.append(part + came.astype(f32))
                parts = sums
            if step < chips:
                parts = [part.astype(bf16) for part in parts]
                running = [chip_ring(x) for x in parts]
        return parts, staged

    first, staged = layer(entering, arriving, where_ready, traded)
    leaving = []
    for i, new in enumerate(in_pieces(fresh[0])):
        if leaving:
            first[i] = after(first[i], leaving)
        leaving.append(jnp.where(position == sections - 1, new, first[i].astype(bf16)))
    ahead = [next_section(x, 1) for x in leaving]
    where_later = ready(where_ready, leaving[0])
    level = [next_section(x, 0) for x in after(leaving, ahead)]
    second, _ = layer(level, ahead, where_later, (), staged)
    return jnp.stack([jnp.concatenate(first, axis=1), jnp.concatenate(second, axis=1)])[None]


def solution(mesh):
    placed = (
        P("section", "seq", None),
        P(None, "seq", None),
        P("section", None, None),
        P("section", None, None, "seq"),
        P("section", None, None),
        P("section", None),
        P("section", None),
        P("section", None),
        P("section", None),
        P("section", None),
        P("section", "seq", None),
    )

    return jax.shard_map(
        on_device,
        mesh=mesh,
        in_specs=placed,
        out_specs=P("section", None, "seq", None),
        check_vma=False,
    )
```

```python
import functools

import jax
import jax.numpy as jnp
from jax import lax
from jax.experimental import pallas as pl
from jax.experimental.pallas import tpu as pltpu
from jax.sharding import PartitionSpec as P


HEADS = 128
HEAD_DIM = 32
STATE = 64
GROUPS = 4
CONV = 4
BLOCK = 128
LANES = 128
PIECES = 2
QUAD = LANES // HEAD_DIM


bf16 = jnp.bfloat16
f32 = jnp.float32


def swapped(value, bit):
    count = lax.axis_size("seq")
    return lax.ppermute(value, "seq", [(i, i ^ bit) for i in range(count)])


def chip_ring(value):
    count = lax.axis_size("seq")
    return lax.ppermute(value, "seq", [(i, (i + 2) % count) for i in range(count)])


def next_section(value, chips_on):
    sections, count = lax.axis_size("section"), lax.axis_size("seq")
    pairs = [
        (s * count + i, (s + 1) % sections * count + (i + 2 * chips_on) % count)
        for s in range(sections)
        for i in range(count)
    ]
    return lax.ppermute(value, ("section", "seq"), pairs)


IN_VMEM = pl.BlockSpec(memory_space=pltpu.VMEM)
IN_SMEM = pl.BlockSpec(memory_space=pltpu.SMEM)
PARAMS = pltpu.CompilerParams(vmem_limit_bytes=16 * 1024 * 1024)


def after(values, *others):
    return lax.optimization_barrier((values, others))[0]


def chip_at(where, steps, chips):
    return lax.rem(where[0] + (chips - steps), chips)


def project_kernel(where, *refs, steps, chips):
    xs, refs = refs[: 2 * PIECES], refs[2 * PIECES :]
    xz_parts, p_weight, outs = refs[:PIECES], refs[PIECES], refs[-2:]
    core = where[1]
    tokens, depth = xs[0].shape
    start = chip_at(where, steps, chips) * (2 * tokens)
    mine = pl.ds(pl.multiple_of(start + core * tokens, tokens), tokens)
    other = pl.ds(pl.multiple_of(start + (1 - core) * tokens, tokens), tokens)
    tall = [
        jnp.concatenate([xs[i][...], xs[PIECES + i][...]], axis=0) for i in range(PIECES)
    ]
    p_parts = [p_weight.at[i * depth : (i + 1) * depth, :] for i in range(PIECES)]
    for weights, out in zip((xz_parts, p_parts), outs):
        total = None
        for x, weight in zip(tall, weights):
            part = jnp.dot(x, weight[...], preferred_element_type=f32)
            total = part if total is None else total + part
        total = total.astype(bf16)
        out[mine, :] = total[:tokens]
        out[other, :] = total[tokens:]


def project(where, steps, chips, xs, weights, length, buffers):
    args = [where, *xs, *weights]
    in_specs = [IN_SMEM] + [IN_VMEM] * (len(args) - 1)
    aliases = {}
    if buffers is not None:
        aliases = {len(args): 0, len(args) + 1: 1}
        args += list(buffers)
        in_specs += [IN_VMEM] * 2
    width = weights[-1].shape[0]
    n_out = [weights[0].shape[1], weights[-1].shape[1]]
    columns = sum(n_out)
    return pl.pallas_call(
        functools.partial(project_kernel, steps=steps, chips=chips),
        in_specs=in_specs,
        out_specs=[IN_VMEM] * 2,
        out_shape=[jax.ShapeDtypeStruct((length, n), bf16) for n in n_out],
        input_output_aliases=aliases,
        compiler_params=PARAMS,
        cost_estimate=pl.CostEstimate(
            flops=2 * (length // chips) * width * columns,
            bytes_accessed=2 * width * columns,
            transcendentals=0,
        ),
        name="project",
    )(*args)


def ready_kernel(where, weight, out):
    del weight
    out[0] = where[0]
    out[1] = where[1]


def ready(where, weight):
    return pl.pallas_call(
        ready_kernel,
        in_specs=[IN_SMEM, pl.BlockSpec(memory_space=pl.ANY)],
        out_specs=IN_SMEM,
        out_shape=jax.ShapeDtypeStruct(where.shape, where.dtype),
        compiler_params=PARAMS,
        name="ready",
    )(where, weight)


def stage_kernel(upper, lower, out, semaphores):
    rows = upper.shape[0]
    copies = [
        pltpu.make_async_copy(part, out.at[i * rows : (i + 1) * rows, :], semaphores.at[i])
        for i, part in enumerate((upper, lower))
    ]
    for copy in copies:
        copy.start()
    for copy in copies:
        copy.wait()


def stage(upper, lower):
    rows, cols = upper.shape
    return pl.pallas_call(
        stage_kernel,
        in_specs=[pl.BlockSpec(memory_space=pl.ANY)] * 2,
        out_specs=IN_VMEM,
        out_shape=jax.ShapeDtypeStruct((2 * rows, cols), upper.dtype),
        scratch_shapes=[pltpu.SemaphoreType.DMA((2,))],
        compiler_params=PARAMS,
        cost_estimate=pl.CostEstimate(
            flops=0, bytes_accessed=8 * rows * cols, transcendentals=0
        ),
        name="stage",
    )(upper, lower)


def spread_of(chans):
    return (
        lax.broadcasted_iota(jnp.int32, (LANES, chans), 0)
        == lax.broadcasted_iota(jnp.int32, (LANES, chans), 1) // HEAD_DIM
    )


def tables_kernel(
    where, conv_w, conv_b, step_b, decay, skip_w, norm_g,
    taps, offset, bias, rate, skip, gain,
):
    chans = gain.shape[1]
    heads = chans // HEAD_DIM
    member = where[0] * 2 + where[1]
    first = member * heads
    group = first // (HEADS // GROUPS)
    odd = lax.rem(group, 2) == 1
    own = pl.ds(pl.multiple_of(member * chans, LANES), chans)
    inner = HEADS * HEAD_DIM
    for table, out in ((conv_w, taps), (conv_b, offset)):
        out[:, :chans] = table[:, own]
        b_at = pl.multiple_of(inner + group // 2 * LANES, LANES)
        c_at = pl.multiple_of(inner + GROUPS * STATE + group // 2 * LANES, LANES)
        count = table.shape[0]
        rows = []
        for k in range(count):
            b = jnp.broadcast_to(table[k : k + 1, pl.ds(b_at, LANES)], (8, LANES))
            c = jnp.broadcast_to(table[k : k + 1, pl.ds(c_at, LANES)], (8, LANES))
            b = jnp.where(odd, pltpu.roll(b, STATE, 1), b)
            c = jnp.where(odd, c, pltpu.roll(c, STATE, 1))
            lane = lax.broadcasted_iota(jnp.int32, (8, LANES), 1)
            rows.append(jnp.where(lane < STATE, b, c)[0:1])
        for k in range(count):
            out[k : k + 1, chans:] = rows[k]
    back = lax.rem(HEADS - first, HEADS)

    def own_heads(table):
        return pltpu.roll(jnp.broadcast_to(table[...], (8, LANES)), back, 1)

    bias[...] = own_heads(step_b)[0:1]
    rate[...] = -jnp.exp(own_heads(decay)[0:1])
    skip[...] = jnp.dot(
        own_heads(skip_w),
        spread_of(chans).astype(f32),
        precision=lax.Precision.HIGHEST,
        preferred_element_type=f32,
    )[0:1]
    gain[...] = norm_g[:, own]


def tables_of(where, params, chans):
    shapes = (
        (CONV, chans + 2 * STATE), (1, chans + 2 * STATE), (1, LANES), (1, LANES), (1, chans),
        (1, chans),
    )
    return pl.pallas_call(
        tables_kernel,
        in_specs=[IN_SMEM] + [IN_VMEM] * len(params),
        out_specs=[IN_VMEM] * len(shapes),
        out_shape=[jax.ShapeDtypeStruct(shape, f32) for shape in shapes],
        compiler_params=PARAMS,
        name="tables",
    )(where, *params)


def silu(value):
    half = 0.5 * value
    return half + half * jnp.tanh(half)


def split_terms(value, terms):
    parts = []
    for _ in range(terms - 1):
        parts.append(value.astype(bf16))
        value = value - parts[-1].astype(f32)
    return parts + [value.astype(bf16)]


def mix_kernel(
    where, xz_ref, p_ref, taps_ref, offset_ref, bias_ref, rate_ref, skip_ref, gain_ref,
    mine_ref, theirs_ref, mine_squares, theirs_squares,
    tail_ref, state_ref, gated_ref, squares_ref,
):
    chans = mine_ref.shape[1]
    heads = chans // HEAD_DIM
    rows = pl.ds(pl.multiple_of(pl.program_id(0) * BLOCK, BLOCK), BLOCK)

    @pl.when(pl.program_id(0) == 0)
    def _():
        tail_ref[...] = jnp.zeros_like(tail_ref)
        state_ref[...] = jnp.zeros_like(state_ref)

    joined = jnp.concatenate(
        [xz_ref[rows, chans:].astype(f32), p_ref[rows, 0 : 2 * STATE].astype(f32)], axis=1
    )
    lead = tail_ref.shape[0]
    tail = tail_ref[...]
    top = lax.broadcasted_iota(jnp.int32, tail.shape, 0)
    total = offset_ref[0:1, :] + taps_ref[CONV - 1 : CONV, :] * joined
    for back in range(1, CONV):
        rolled = pltpu.roll(joined, back, 0)
        first = jnp.where(top < back, pltpu.roll(tail, back, 0), rolled[:lead])
        moved = jnp.concatenate([first, rolled[lead:]], axis=0)
        total = total + taps_ref[CONV - 1 - back : CONV - back, :] * moved
    tail_ref[...] = joined[BLOCK - lead :]
    convolved = silu(total).astype(bf16)
    x = convolved[:, :chans]
    bc = convolved[:, chans:]
    b = bc[:, :STATE]
    c = bc[:, STATE:]

    step = jax.nn.softplus(p_ref[rows, 2 * STATE :].astype(f32) + bias_ref[0:1, :])
    decay = rate_ref[0:1, :] * step
    row = lax.broadcasted_iota(jnp.int32, (BLOCK, BLOCK), 0)
    col = lax.broadcasted_iota(jnp.int32, (BLOCK, BLOCK), 1)
    lower = row >= col
    terms = split_terms(decay, 3)
    cumulus = jnp.dot(
        jnp.concatenate([lower.astype(bf16)] * len(terms), axis=1),
        jnp.concatenate(terms, axis=0),
        preferred_element_type=f32,
    )
    block_total = cumulus[BLOCK - 1 : BLOCK, :]
    lowered_t = (cumulus - jnp.log(step)).T
    scores = lax.dot_general(c, b, (((1,), (1,)), ((), ())), preferred_element_type=f32)
    spread = spread_of(chans).astype(bf16)
    spread = jnp.concatenate([spread, spread], axis=0)

    def per_channel(table):
        return jnp.dot(
            jnp.concatenate(split_terms(table, 2), axis=1), spread, preferred_element_type=f32
        )

    grown = per_channel(jnp.exp(cumulus))
    kept = per_channel(jnp.exp(block_total - cumulus) * step)
    x_wide = x.astype(f32)
    weighted = (x_wide * kept).astype(bf16)
    entering = state_ref[...].astype(bf16)
    carried = jnp.dot(c, entering, preferred_element_type=f32) * grown
    block_state = lax.dot_general(
        b, weighted, (((0,), (0,)), ((), ())), preferred_element_type=f32
    )
    state_ref[...] = grown[BLOCK - 1 : BLOCK, :] * state_ref[...] + block_state

    lane_head = lax.broadcasted_iota(jnp.int32, (BLOCK, LANES), 1) // HEAD_DIM
    squares = jnp.zeros((BLOCK, 1), f32)
    for quad in range(heads // QUAD):
        lanes = slice(quad * LANES, (quad + 1) * LANES)
        x_quad = x[:, lanes]
        left, right = [], []
        for j in range(QUAD):
            h = quad * QUAD + j
            gap = jnp.where(lower, cumulus[:, h : h + 1] - lowered_t[h : h + 1, :], -1e30)
            left.append((scores * jnp.exp(gap)).astype(bf16))
            right.append(jnp.where(lane_head == j, x_quad, jnp.zeros_like(x_quad)))
        diagonal = jnp.dot(
            jnp.concatenate(left, axis=1),
            jnp.concatenate(right, axis=0),
            preferred_element_type=f32,
        )
        mixed = diagonal + carried[:, lanes] + skip_ref[0:1, lanes] * x_wide[:, lanes]
        gated = mixed * silu(xz_ref[rows, lanes].astype(f32))
        squares = squares + jnp.sum(gated * gated, axis=1, keepdims=True)
        gated_ref[:, lanes] = (gated * gain_ref[0:1, lanes]).astype(bf16)
    squares_ref[...] = jnp.broadcast_to(squares, (BLOCK, LANES))
    part = BLOCK // 2
    core = where[1]
    to = pl.ds(pl.multiple_of(pl.program_id(0) * part, part), part)
    near = pl.ds(pl.multiple_of(core * part, part), part)
    far = pl.ds(pl.multiple_of((1 - core) * part, part), part)
    mine_ref[to, :] = gated_ref[near, :]
    theirs_ref[to, :] = gated_ref[far, :]
    mine_squares[to, :] = squares_ref[near, :]
    theirs_squares[to, :] = squares_ref[far, :]


def mix(where, xz, p, tables):
    length, both = xz.shape
    chans = both // 2
    n_p = p.shape[1]
    return pl.pallas_call(
        mix_kernel,
        grid=(length // BLOCK,),
        in_specs=[IN_SMEM] + [IN_VMEM] * (2 + len(tables)),
        out_specs=[IN_VMEM] * 4,
        compiler_params=PARAMS,
        out_shape=[jax.ShapeDtypeStruct((length // 2, chans), bf16)] * 2
        + [jax.ShapeDtypeStruct((length // 2, LANES), f32)] * 2,
        scratch_shapes=[
            pltpu.VMEM((8, chans + 2 * STATE), f32),
            pltpu.VMEM((STATE, chans), f32),
            pltpu.VMEM((BLOCK, chans), bf16),
            pltpu.VMEM((BLOCK, LANES), f32),
        ],
        cost_estimate=pl.CostEstimate(
            flops=2 * length * chans * BLOCK * 8,
            bytes_accessed=2 * length * (both + chans + n_p),
            transcendentals=length * chans * 4,
        ),
        name="mix",
    )(where, xz, p, *tables)


def out_kernel(where, g_mine, g_other, weight, *refs, steps, chips, first, count, scale):
    squares, outs = refs[:-count], refs[-count:]
    rows, tile = outs[0].shape
    at = pl.ds(pl.multiple_of(chip_at(where, steps, chips) * rows, rows), rows)
    total = squares[0][at, 0:1]
    for more in squares[1:]:
        total = total + more[at, 0:1]
    rate = lax.rsqrt(total * scale + 1e-05)
    both = jnp.concatenate([g_mine[at, :], g_other[at, :]], axis=1)
    for i, out in enumerate(outs):
        cols = slice((first + i) * tile, (first + i + 1) * tile)
        part = jnp.dot(both, weight[:, cols], preferred_element_type=f32)
        out[...] = (part * rate).astype(out.dtype)


def out_project(where, steps, chips, gated, weight, squares, pieces, dtype):
    chans, cols = weight.shape
    rows = gated[0].shape[0] // chips
    first, count = pieces
    args = [where, *gated, weight, *squares]
    return pl.pallas_call(
        functools.partial(
            out_kernel,
            steps=steps,
            chips=chips,
            first=first,
            count=count,
            scale=GROUPS / (HEADS * HEAD_DIM),
        ),
        in_specs=[IN_SMEM] + [IN_VMEM] * (len(args) - 1),
        out_specs=[IN_VMEM] * count,
        out_shape=[jax.ShapeDtypeStruct((rows, cols // PIECES), dtype)] * count,
        compiler_params=PARAMS,
        cost_estimate=pl.CostEstimate(
            flops=2 * rows * chans * cols * count // PIECES,
            bytes_accessed=2 * chans * cols * count // PIECES,
            transcendentals=0,
        ),
        name="out_project",
    )(*args)


def on_device(
    inflow,
    fresh,
    proj_weight,
    xz_weight,
    conv_weight,
    conv_bias,
    step_bias,
    decay_log,
    skip_weight,
    norm_gain,
    out_weight,
):
    members = lax.axis_size("seq")
    sections = lax.axis_size("section")
    position = lax.axis_index("section")
    member = lax.axis_index("seq")
    chips = members // 2
    tokens, width = inflow.shape[1], inflow.shape[2]
    assert 2 * tokens == BLOCK
    length = tokens * members
    piece = width // PIECES
    heads_dev = HEADS // members
    chan_dev = heads_dev * HEAD_DIM
    bc_width = GROUPS * STATE
    group_members = members // GROUPS
    head_start = member * heads_dev
    group_index = head_start // (HEADS // GROUPS)
    where = jnp.stack([member // 2, member % 2]).astype(jnp.int32)

    def in_pieces(shard):
        return [shard[:, i * piece : (i + 1) * piece] for i in range(PIECES)]

    entering = in_pieces(inflow[0])
    traded = [swapped(entering[0], 1)]
    arriving = []
    for i, x in enumerate(entering):
        x = after(x, traded) if i else x
        arriving.append(chip_ring(x))

    def regrouped(weight, i):
        rows = slice(i * piece, (i + 1) * piece)
        return weight[0, rows].reshape(piece, 2 * chan_dev)

    xz_parts = [regrouped(xz_weight, 0)]
    column = lax.broadcasted_iota(jnp.int32, (proj_weight.shape[2], 2 * LANES), 1)
    source = jnp.where(
        column < STATE,
        group_index * STATE + column,
        jnp.where(
            column < 2 * STATE,
            bc_width + group_index * STATE + column - STATE,
            2 * bc_width + head_start + column - 2 * STATE,
        ),
    )
    chosen = (lax.broadcasted_iota(jnp.int32, column.shape, 0) == source) & (
        column < 2 * STATE + heads_dev
    )
    where_ready = ready(where, xz_parts[0])
    p_local = jnp.dot(
        after(proj_weight[0], where_ready), chosen.astype(bf16), preferred_element_type=f32
    ).astype(bf16)
    xz_parts += [regrouped(after(xz_weight, where_ready), i) for i in range(1, PIECES)]
    tables = tables_of(
        where_ready, (conv_weight[0], conv_bias, step_bias, decay_log, skip_weight, norm_gain), chan_dev
    )
    out_swapped = swapped(out_weight[0], 1)

    def layer(held, arriving, where_ready, traded=(), staged=None):
        traded = list(traded)
        buffers = None
        indices = where_ready
        pausing = staged is not None
        for step in range(chips):
            if step == chips - 1 and staged is None:
                staged = stage(after(out_weight[0], buffers), out_swapped)
            if step == 1:
                held = arriving
            elif step > 1:
                if pausing:
                    indices = ready(indices, held[0])
                held = [chip_ring(x) for x in held]
            other = [swapped(part, 1) for part in held[len(traded) :]]
            other, traded = traded + other, []
            buffers = project(
                indices, step, chips, held + other, (*xz_parts, p_local), length, buffers
            )
        near, far, near_squares, far_squares = mix(where, *buffers, tables)
        gated = (near, swapped(far, 1))
        squares = []
        for mask in range(0, group_members, 2):
            squares.append(swapped(near_squares, mask) if mask else near_squares)
            squares.append(swapped(far_squares, mask ^ 1))
        running = parts = None
        for step in range(1, chips + 1):
            gate = where if parts is None else after(where, parts)
            calls = [(i, 1) for i in range(PIECES)] if step == 1 else [(0, PIECES)]
            parts = []
            for call in calls:
                parts += out_project(
                    after(gate, parts) if parts else gate, step, chips, gated, staged, squares, call,
                    bf16 if step == 1 else f32,
                )
            if running is not None:
                sums = []
                for part, came in zip(parts, running):
                    came = after(came, sums) if sums else came
                    sums.append(part + came.astype(f32))
                parts = sums
            if step < chips:
                parts = [part.astype(bf16) for part in parts]
                running = [chip_ring(x) for x in parts]
        return parts, staged

    first, staged = layer(entering, arriving, where_ready, traded)
    leaving = []
    for i, new in enumerate(in_pieces(fresh[0])):
        if leaving:
            first[i] = after(first[i], leaving)
        leaving.append(jnp.where(position == sections - 1, new, first[i].astype(bf16)))
    ahead = [next_section(x, 1) for x in leaving]
    where_later = ready(where_ready, leaving[0])
    level = [next_section(x, 0) for x in after(leaving, ahead)]
    second, _ = layer(level, ahead, where_later, (), staged)
    return jnp.stack([jnp.concatenate(first, axis=1), jnp.concatenate(second, axis=1)])[None]


def solution(mesh):
    placed = (
        P("section", "seq", None),
        P(None, "seq", None),
        P("section", None, None),
        P("section", None, None, "seq"),
        P("section", None, None),
        P("section", None),
        P("section", None),
        P("section", None),
        P("section", None),
        P("section", None),
        P("section", "seq", None),
    )

    return jax.shard_map(
        on_device,
        mesh=mesh,
        in_specs=placed,
        out_specs=P("section", None, "seq", None),
        check_vma=False,
    )
```

```python
import functools

import jax
import jax.numpy as jnp
from jax import lax
from jax.experimental import pallas as pl
from jax.experimental.pallas import tpu as pltpu
from jax.sharding import PartitionSpec as P


HEADS = 128
HEAD_DIM = 32
STATE = 64
GROUPS = 4
CONV = 4
BLOCK = 128
LANES = 128
PIECES = 2
MERGED = 2
QUAD = LANES // HEAD_DIM


bf16 = jnp.bfloat16
f32 = jnp.float32


def swapped(value, bit):
    count = lax.axis_size("seq")
    return lax.ppermute(value, "seq", [(i, i ^ bit) for i in range(count)])


def chip_ring(value):
    count = lax.axis_size("seq")
    return lax.ppermute(value, "seq", [(i, (i + 2) % count) for i in range(count)])


def next_section(value, chips_on):
    sections, count = lax.axis_size("section"), lax.axis_size("seq")
    pairs = [
        (s * count + i, (s + 1) % sections * count + (i + 2 * chips_on) % count)
        for s in range(sections)
        for i in range(count)
    ]
    return lax.ppermute(value, ("section", "seq"), pairs)


IN_VMEM = pl.BlockSpec(memory_space=pltpu.VMEM)
IN_SMEM = pl.BlockSpec(memory_space=pltpu.SMEM)
PARAMS = pltpu.CompilerParams(vmem_limit_bytes=16 * 1024 * 1024)


def after(values, *others):
    return lax.optimization_barrier((values, others))[0]


def chip_at(where, steps, chips):
    return lax.rem(where[0] + (chips - steps), chips)


def sums_of(xs, xz_parts, p_weight, first):
    count = len(xz_parts)
    depth = xs[0].shape[1]
    tall = [jnp.concatenate([xs[i][...], xs[count + i][...]], axis=0) for i in range(count)]
    p_parts = [p_weight.at[i * depth : (i + 1) * depth, :] for i in range(first, first + count)]
    sums = []
    for weights in (xz_parts, p_parts):
        total = None
        for x, weight in zip(tall, weights):
            part = jnp.dot(x, weight[...], preferred_element_type=f32)
            total = part if total is None else total + part
        sums.append(total)
    return sums


def early_kernel(*refs, count):
    xs, xz_parts, p_weight = refs[: 2 * count], refs[2 * count : 3 * count], refs[3 * count]
    for out, total in zip(refs[-2:], sums_of(xs, xz_parts, p_weight, 0)):
        out[...] = total


def project_early(xs, xz_parts, p_weight):
    count = len(xz_parts)
    rows, depth = 2 * xs[0].shape[0], xs[0].shape[1]
    n_out = [xz_parts[0].shape[1], p_weight.shape[1]]
    args = [*xs, *xz_parts, p_weight]
    return pl.pallas_call(
        functools.partial(early_kernel, count=count),
        in_specs=[IN_VMEM] * len(args),
        out_specs=[IN_VMEM] * 2,
        out_shape=[jax.ShapeDtypeStruct((rows, n), f32) for n in n_out],
        compiler_params=PARAMS,
        cost_estimate=pl.CostEstimate(
            flops=2 * rows * depth * count * sum(n_out),
            bytes_accessed=2 * depth * count * sum(n_out),
            transcendentals=0,
        ),
        name="project_early",
    )(*args)


def project_kernel(where, *refs, steps, chips, first, has_early):
    count = PIECES - first
    xs, refs = refs[: 2 * count], refs[2 * count :]
    xz_parts, p_weight, outs = refs[:count], refs[count], refs[-2:]
    core = where[1]
    tokens = xs[0].shape[0]
    start = chip_at(where, steps, chips) * (2 * tokens)
    mine = pl.ds(pl.multiple_of(start + core * tokens, tokens), tokens)
    other = pl.ds(pl.multiple_of(start + (1 - core) * tokens, tokens), tokens)
    for i, (out, total) in enumerate(zip(outs, sums_of(xs, xz_parts, p_weight, first))):
        if has_early:
            total = total + refs[count + 1 + i][...]
        total = total.astype(bf16)
        out[mine, :] = total[:tokens]
        out[other, :] = total[tokens:]


def project(where, steps, chips, xs, xz_parts, p_weight, length, buffers, early=()):
    args = [where, *xs, *xz_parts, p_weight, *early]
    in_specs = [IN_SMEM] + [IN_VMEM] * (len(args) - 1)
    aliases = {}
    if buffers is not None:
        aliases = {len(args): 0, len(args) + 1: 1}
        args += list(buffers)
        in_specs += [IN_VMEM] * 2
    depth = xs[0].shape[1] * len(xz_parts)
    n_out = [xz_parts[0].shape[1], p_weight.shape[1]]
    return pl.pallas_call(
        functools.partial(
            project_kernel,
            steps=steps,
            chips=chips,
            first=PIECES - len(xz_parts),
            has_early=bool(early),
        ),
        in_specs=in_specs,
        out_specs=[IN_VMEM] * 2,
        out_shape=[jax.ShapeDtypeStruct((length, n), bf16) for n in n_out],
        input_output_aliases=aliases,
        compiler_params=PARAMS,
        cost_estimate=pl.CostEstimate(
            flops=2 * (length // chips) * depth * sum(n_out),
            bytes_accessed=2 * depth * sum(n_out),
            transcendentals=0,
        ),
        name="project",
    )(*args)


def ready_kernel(where, weight, out):
    del weight
    out[0] = where[0]
    out[1] = where[1]


def ready(where, weight):
    return pl.pallas_call(
        ready_kernel,
        in_specs=[IN_SMEM, pl.BlockSpec(memory_space=pl.ANY)],
        out_specs=IN_SMEM,
        out_shape=jax.ShapeDtypeStruct(where.shape, where.dtype),
        compiler_params=PARAMS,
        name="ready",
    )(where, weight)


def stage_kernel(upper, lower, out, semaphores):
    rows = upper.shape[0]
    copies = [
        pltpu.make_async_copy(part, out.at[i * rows : (i + 1) * rows, :], semaphores.at[i])
        for i, part in enumerate((upper, lower))
    ]
    for copy in copies:
        copy.start()
    for copy in copies:
        copy.wait()


def stage(upper, lower):
    rows, cols = upper.shape
    return pl.pallas_call(
        stage_kernel,
        in_specs=[pl.BlockSpec(memory_space=pl.ANY)] * 2,
        out_specs=IN_VMEM,
        out_shape=jax.ShapeDtypeStruct((2 * rows, cols), upper.dtype),
        scratch_shapes=[pltpu.SemaphoreType.DMA((2,))],
        compiler_params=PARAMS,
        cost_estimate=pl.CostEstimate(
            flops=0, bytes_accessed=8 * rows * cols, transcendentals=0
        ),
        name="stage",
    )(upper, lower)


def spread_of(chans):
    return (
        lax.broadcasted_iota(jnp.int32, (LANES, chans), 0)
        == lax.broadcasted_iota(jnp.int32, (LANES, chans), 1) // HEAD_DIM
    )


def tables_kernel(
    where, conv_w, conv_b, step_b, decay, skip_w, norm_g,
    taps, offset, bias, rate, skip, gain,
):
    chans = gain.shape[1]
    heads = chans // HEAD_DIM
    member = where[0] * 2 + where[1]
    first = member * heads
    group = first // (HEADS // GROUPS)
    odd = lax.rem(group, 2) == 1
    own = pl.ds(pl.multiple_of(member * chans, LANES), chans)
    inner = HEADS * HEAD_DIM
    for table, out in ((conv_w, taps), (conv_b, offset)):
        out[:, :chans] = table[:, own]
        b_at = pl.multiple_of(inner + group // 2 * LANES, LANES)
        c_at = pl.multiple_of(inner + GROUPS * STATE + group // 2 * LANES, LANES)
        count = table.shape[0]
        rows = []
        for k in range(count):
            b = jnp.broadcast_to(table[k : k + 1, pl.ds(b_at, LANES)], (8, LANES))
            c = jnp.broadcast_to(table[k : k + 1, pl.ds(c_at, LANES)], (8, LANES))
            b = jnp.where(odd, pltpu.roll(b, STATE, 1), b)
            c = jnp.where(odd, c, pltpu.roll(c, STATE, 1))
            lane = lax.broadcasted_iota(jnp.int32, (8, LANES), 1)
            rows.append(jnp.where(lane < STATE, b, c)[0:1])
        for k in range(count):
            out[k : k + 1, chans:] = rows[k]
    back = lax.rem(HEADS - first, HEADS)

    def own_heads(table):
        return pltpu.roll(jnp.broadcast_to(table[...], (8, LANES)), back, 1)

    bias[...] = own_heads(step_b)[0:1]
    rate[...] = -jnp.exp(own_heads(decay)[0:1])
    skip[...] = jnp.dot(
        own_heads(skip_w),
        spread_of(chans).astype(f32),
        precision=lax.Precision.HIGHEST,
        preferred_element_type=f32,
    )[0:1]
    gain[...] = norm_g[:, own]


def tables_of(where, params, chans):
    shapes = (
        (CONV, chans + 2 * STATE), (1, chans + 2 * STATE), (1, LANES), (1, LANES), (1, chans),
        (1, chans),
    )
    return pl.pallas_call(
        tables_kernel,
        in_specs=[IN_SMEM] + [IN_VMEM] * len(params),
        out_specs=[IN_VMEM] * len(shapes),
        out_shape=[jax.ShapeDtypeStruct(shape, f32) for shape in shapes],
        compiler_params=PARAMS,
        name="tables",
    )(where, *params)


def silu(value):
    half = 0.5 * value
    return half + half * jnp.tanh(half)


def split_terms(value, terms):
    parts = []
    for _ in range(terms - 1):
        parts.append(value.astype(bf16))
        value = value - parts[-1].astype(f32)
    return parts + [value.astype(bf16)]


def mix_kernel(*refs):
    tail_ref, state_ref = refs[-4:-2]

    @pl.when(pl.program_id(0) == 0)
    def _():
        tail_ref[...] = jnp.zeros_like(tail_ref)
        state_ref[...] = jnp.zeros_like(state_ref)

    for i in range(MERGED):
        mix_block(pl.program_id(0) * MERGED + i, *refs[:-2], refs[-2].at[i], refs[-1].at[i])


def mix_block(
    block, where, xz_ref, p_ref, taps_ref, offset_ref, bias_ref, rate_ref, skip_ref, gain_ref,
    mine_ref, theirs_ref, mine_squares, theirs_squares,
    tail_ref, state_ref, gated_ref, squares_ref,
):
    chans = mine_ref.shape[1]
    heads = chans // HEAD_DIM
    rows = pl.ds(pl.multiple_of(block * BLOCK, BLOCK), BLOCK)

    joined = jnp.concatenate(
        [xz_ref[rows, chans:].astype(f32), p_ref[rows, 0 : 2 * STATE].astype(f32)], axis=1
    )
    lead = tail_ref.shape[0]
    tail = tail_ref[...]
    top = lax.broadcasted_iota(jnp.int32, tail.shape, 0)
    total = offset_ref[0:1, :] + taps_ref[CONV - 1 : CONV, :] * joined
    for back in range(1, CONV):
        rolled = pltpu.roll(joined, back, 0)
        first = jnp.where(top < back, pltpu.roll(tail, back, 0), rolled[:lead])
        moved = jnp.concatenate([first, rolled[lead:]], axis=0)
        total = total + taps_ref[CONV - 1 - back : CONV - back, :] * moved
    tail_ref[...] = joined[BLOCK - lead :]
    convolved = silu(total).astype(bf16)
    x = convolved[:, :chans]
    bc = convolved[:, chans:]
    b = bc[:, :STATE]
    c = bc[:, STATE:]

    step = jax.nn.softplus(p_ref[rows, 2 * STATE :].astype(f32) + bias_ref[0:1, :])
    decay = rate_ref[0:1, :] * step
    row = lax.broadcasted_iota(jnp.int32, (BLOCK, BLOCK), 0)
    col = lax.broadcasted_iota(jnp.int32, (BLOCK, BLOCK), 1)
    lower = row >= col
    terms = split_terms(decay, 3)
    cumulus = jnp.dot(
        jnp.concatenate([lower.astype(bf16)] * len(terms), axis=1),
        jnp.concatenate(terms, axis=0),
        preferred_element_type=f32,
    )
    block_total = cumulus[BLOCK - 1 : BLOCK, :]
    lowered_t = (cumulus - jnp.log(step)).T
    scores = lax.dot_general(c, b, (((1,), (1,)), ((), ())), preferred_element_type=f32)
    spread = spread_of(chans).astype(bf16)
    spread = jnp.concatenate([spread, spread], axis=0)

    def per_channel(table):
        return jnp.dot(
            jnp.concatenate(split_terms(table, 2), axis=1), spread, preferred_element_type=f32
        )

    grown = per_channel(jnp.exp(cumulus))
    kept = per_channel(jnp.exp(block_total - cumulus) * step)
    x_wide = x.astype(f32)
    weighted = (x_wide * kept).astype(bf16)
    entering = state_ref[...].astype(bf16)
    carried = jnp.dot(c, entering, preferred_element_type=f32) * grown
    block_state = lax.dot_general(
        b, weighted, (((0,), (0,)), ((), ())), preferred_element_type=f32
    )
    state_ref[...] = grown[BLOCK - 1 : BLOCK, :] * state_ref[...] + block_state

    lane_head = lax.broadcasted_iota(jnp.int32, (BLOCK, LANES), 1) // HEAD_DIM
    squares = jnp.zeros((BLOCK, 1), f32)
    for quad in range(heads // QUAD):
        lanes = slice(quad * LANES, (quad + 1) * LANES)
        x_quad = x[:, lanes]
        left, right = [], []
        for j in range(QUAD):
            h = quad * QUAD + j
            gap = jnp.where(lower, cumulus[:, h : h + 1] - lowered_t[h : h + 1, :], -1e30)
            left.append((scores * jnp.exp(gap)).astype(bf16))
            right.append(jnp.where(lane_head == j, x_quad, jnp.zeros_like(x_quad)))
        diagonal = jnp.dot(
            jnp.concatenate(left, axis=1),
            jnp.concatenate(right, axis=0),
            preferred_element_type=f32,
        )
        mixed = diagonal + carried[:, lanes] + skip_ref[0:1, lanes] * x_wide[:, lanes]
        gated = mixed * silu(xz_ref[rows, lanes].astype(f32))
        squares = squares + jnp.sum(gated * gated, axis=1, keepdims=True)
        gated_ref[:, lanes] = (gated * gain_ref[0:1, lanes]).astype(bf16)
    squares_ref[...] = jnp.broadcast_to(squares, (BLOCK, LANES))
    part = BLOCK // 2
    core = where[1]
    to = pl.ds(pl.multiple_of(block * part, part), part)
    near = pl.ds(pl.multiple_of(core * part, part), part)
    far = pl.ds(pl.multiple_of((1 - core) * part, part), part)
    mine_ref[to, :] = gated_ref[near, :]
    theirs_ref[to, :] = gated_ref[far, :]
    mine_squares[to, :] = squares_ref[near, :]
    theirs_squares[to, :] = squares_ref[far, :]


def mix(where, xz, p, tables):
    length, both = xz.shape
    chans = both // 2
    n_p = p.shape[1]
    return pl.pallas_call(
        mix_kernel,
        grid=(length // BLOCK // MERGED,),
        in_specs=[IN_SMEM] + [IN_VMEM] * (2 + len(tables)),
        out_specs=[IN_VMEM] * 4,
        compiler_params=PARAMS,
        out_shape=[jax.ShapeDtypeStruct((length // 2, chans), bf16)] * 2
        + [jax.ShapeDtypeStruct((length // 2, LANES), f32)] * 2,
        scratch_shapes=[
            pltpu.VMEM((8, chans + 2 * STATE), f32),
            pltpu.VMEM((STATE, chans), f32),
            pltpu.VMEM((MERGED, BLOCK, chans), bf16),
            pltpu.VMEM((MERGED, BLOCK, LANES), f32),
        ],
        cost_estimate=pl.CostEstimate(
            flops=2 * length * chans * BLOCK * 8,
            bytes_accessed=2 * length * (both + chans + n_p),
            transcendentals=length * chans * 4,
        ),
        name="mix",
    )(where, xz, p, *tables)


def out_kernel(where, g_mine, g_other, weight, *refs, steps, chips, first, count, scale):
    squares, outs = refs[:-count], refs[-count:]
    rows, tile = outs[0].shape
    at = pl.ds(pl.multiple_of(chip_at(where, steps, chips) * rows, rows), rows)
    total = squares[0][at, 0:1]
    for more in squares[1:]:
        total = total + more[at, 0:1]
    rate = lax.rsqrt(total * scale + 1e-05)
    both = jnp.concatenate([g_mine[at, :], g_other[at, :]], axis=1)
    for i, out in enumerate(outs):
        cols = slice((first + i) * tile, (first + i + 1) * tile)
        part = jnp.dot(both, weight[:, cols], preferred_element_type=f32)
        out[...] = (part * rate).astype(out.dtype)


def out_project(where, steps, chips, gated, weight, squares, pieces, dtype):
    chans, cols = weight.shape
    rows = gated[0].shape[0] // chips
    first, count = pieces
    args = [where, *gated, weight, *squares]
    return pl.pallas_call(
        functools.partial(
            out_kernel,
            steps=steps,
            chips=chips,
            first=first,
            count=count,
            scale=GROUPS / (HEADS * HEAD_DIM),
        ),
        in_specs=[IN_SMEM] + [IN_VMEM] * (len(args) - 1),
        out_specs=[IN_VMEM] * count,
        out_shape=[jax.ShapeDtypeStruct((rows, cols // PIECES), dtype)] * count,
        compiler_params=PARAMS,
        cost_estimate=pl.CostEstimate(
            flops=2 * rows * chans * cols * count // PIECES,
            bytes_accessed=2 * chans * cols * count // PIECES,
            transcendentals=0,
        ),
        name="out_project",
    )(*args)


def on_device(
    inflow,
    fresh,
    proj_weight,
    xz_weight,
    conv_weight,
    conv_bias,
    step_bias,
    decay_log,
    skip_weight,
    norm_gain,
    out_weight,
):
    members = lax.axis_size("seq")
    sections = lax.axis_size("section")
    position = lax.axis_index("section")
    member = lax.axis_index("seq")
    chips = members // 2
    tokens, width = inflow.shape[1], inflow.shape[2]
    assert 2 * tokens == BLOCK
    length = tokens * members
    piece = width // PIECES
    heads_dev = HEADS // members
    chan_dev = heads_dev * HEAD_DIM
    bc_width = GROUPS * STATE
    group_members = members // GROUPS
    head_start = member * heads_dev
    group_index = head_start // (HEADS // GROUPS)
    where = jnp.stack([member // 2, member % 2]).astype(jnp.int32)

    def in_pieces(shard):
        return [shard[:, i * piece : (i + 1) * piece] for i in range(PIECES)]

    entering = in_pieces(inflow[0])
    traded = [swapped(entering[0], 1)]
    arriving = []
    for i, x in enumerate(entering):
        x = after(x, traded) if i else x
        arriving.append(chip_ring(x))

    def regrouped(weight, i):
        rows = slice(i * piece, (i + 1) * piece)
        return weight[0, rows].reshape(piece, 2 * chan_dev)

    xz_parts = [regrouped(xz_weight, 0)]
    column = lax.broadcasted_iota(jnp.int32, (proj_weight.shape[2], 2 * LANES), 1)
    source = jnp.where(
        column < STATE,
        group_index * STATE + column,
        jnp.where(
            column < 2 * STATE,
            bc_width + group_index * STATE + column - STATE,
            2 * bc_width + head_start + column - 2 * STATE,
        ),
    )
    chosen = (lax.broadcasted_iota(jnp.int32, column.shape, 0) == source) & (
        column < 2 * STATE + heads_dev
    )
    where_ready = ready(where, xz_parts[0])
    p_local = jnp.dot(
        after(proj_weight[0], where_ready), chosen.astype(bf16), preferred_element_type=f32
    ).astype(bf16)
    xz_parts += [regrouped(after(xz_weight, where_ready), i) for i in range(1, PIECES)]
    tables = tables_of(
        where_ready,
        (conv_weight[0], conv_bias, step_bias, decay_log, skip_weight, norm_gain),
        chan_dev,
    )
    out_swapped = swapped(out_weight[0], 1)

    def layer(held, arriving, where_ready, traded=(), staged=None):
        traded = list(traded)
        buffers = None
        indices = where_ready
        pausing = staged is not None
        for step in range(chips):
            if step == chips - 1 and staged is None:
                staged = stage(after(out_weight[0], buffers), out_swapped)
            if step == 1:
                held = arriving
            elif step > 1:
                if pausing:
                    indices = ready(indices, held[0])
                held = [chip_ring(x) for x in held]
            other = [swapped(part, 1) for part in held[len(traded) :]]
            other, traded = traded + other, []
            parts_in = xz_parts
            early = ()
            if step == chips - 1:
                early = project_early(held[:-1] + other[:-1], xz_parts[:-1], p_local)
                held, other, parts_in = held[-1:], other[-1:], xz_parts[-1:]
            buffers = project(
                indices, step, chips, held + other, parts_in, p_local, length, buffers, early
            )
        near, far, near_squares, far_squares = mix(where, *buffers, tables)
        gated = (near, swapped(far, 1))
        squares = []
        for mask in range(0, group_members, 2):
            squares.append(swapped(near_squares, mask) if mask else near_squares)
            squares.append(swapped(far_squares, mask ^ 1))
        running = parts = None
        for step in range(1, chips + 1):
            gate = where if parts is None else after(where, parts)
            calls = [(i, 1) for i in range(PIECES)] if step == 1 else [(0, PIECES)]
            parts = []
            for call in calls:
                parts += out_project(
                    after(gate, parts) if parts else gate, step, chips, gated, staged, squares, call,
                    bf16 if step == 1 else f32,
                )
            if running is not None:
                sums = []
                for part, came in zip(parts, running):
                    came = after(came, sums) if sums else came
                    sums.append(part + came.astype(f32))
                parts = sums
            if step < chips:
                parts = [part.astype(bf16) for part in parts]
                running = [chip_ring(x) for x in parts]
        return parts, staged

    first, staged = layer(entering, arriving, where_ready, traded)
    leaving = []
    for i, new in enumerate(in_pieces(fresh[0])):
        if leaving:
            first[i] = after(first[i], leaving)
        leaving.append(jnp.where(position == sections - 1, new, first[i].astype(bf16)))
    ahead = [next_section(x, 1) for x in leaving]
    where_later = ready(where_ready, leaving[0])
    level = [next_section(x, 0) for x in after(leaving, ahead)]
    second, _ = layer(level, ahead, where_later, (), staged)
    done = jnp.concatenate(first, axis=1)[None, None]
    done = jnp.concatenate([done, jnp.zeros_like(done)], axis=1)
    for i, part in enumerate(second):
        done = lax.dynamic_update_slice(done, part[None, None], (0, 1, 0, i * piece))
    return done


def solution(mesh):
    placed = (
        P("section", "seq", None),
        P(None, "seq", None),
        P("section", None, None),
        P("section", None, None, "seq"),
        P("section", None, None),
        P("section", None),
        P("section", None),
        P("section", None),
        P("section", None),
        P("section", None),
        P("section", "seq", None),
    )

    return jax.shard_map(
        on_device,
        mesh=mesh,
        in_specs=placed,
        out_specs=P("section", None, "seq", None),
        check_vma=False,
    )
```
